32 devices in a mesh: slab: 8 (over y, x, core), term: 4 (over z).
Axes of the slice: x: 2, y: 2, z: 4, core: 2. Of those that a mesh axis runs over, the one named last changes fastest.
Arguments:
- panels: float32 [64, 1024], P(None, 'term'), may hold values from -0.1875 to 0.1875
- block_phase: int32 [2, 64], P(None, 'term'), may hold values from 0 to 4194303
- target_owner: int32 [16384, 1], P(('slab', 'term')), may hold values from 0 to 31; in each aligned block of 512 rows (0 to 511, 512 to 1023, ...) at most 32 rows name the same one
- target_cell: int32 [16384], P(('slab', 'term')), may hold values from 0 to 6143
- target_offset: int32 [16384], P(('slab', 'term')), may hold values from 0 to 255
Outputs:
- grid_values: float32 [64, 196608], P(None, ('slab', 'term'))
- target_values: float32 [64, 16384], P(None, ('slab', 'term'))
The draws below stay inside these ranges and needn't reach their ends.
Inputs may be any that keep to these rules, and one draw needn't show every extreme that they name: `target_owner`: among the 512 targets of one device no owner appears more than 32 times, and some owner appears exactly 32 times.
All inputs are finite; a program needn't handle non-finite values.
Results may differ from the reference program's by a relative error of at most 0.0003.
Values sent between devices are 32-bit elements; how exact they have to be, the bound alone decides.
A program may use at most 256 MiB of HBM per device.

```python
import math
import jax
import jax.numpy as jnp
import numpy as np
from jax import lax

CH = 32
ORDER = 16
TAPS = 256
OFFQ = 256
ROOTQ = 2048
GS = 6144
TGT_DEV = 512
PHASEQ = 4194304
BLOCKS = 64
NGRID = 196608
TARGETS = 16384
CAP = 32
DEVICES = 32


def place_ends(entries, rng, low, largest):
    dims = entries.shape
    index_at = [jax.random.randint(jax.random.fold_in(rng, axis), (), 0, dims[axis]) for axis in range(len(dims))]
    entries = entries.at[tuple(index_at)].set(low)
    longest = dims.index(max(dims))
    index_at[longest] = (index_at[longest] + 1) % dims[longest]
    return entries.at[tuple(index_at)].set(largest)


def shard_levels(stream_key, shape, pieces, low, largest):
    def one(axis_at, parts):
        heights = jax.random.uniform(jax.random.fold_in(jax.random.fold_in(stream_key, 6), axis_at), (parts,), jnp.float32, low / len(pieces), largest / len(pieces))
        return jnp.repeat(jnp.exp(heights), shape[axis_at] // parts).reshape((-1,) + (1,) * (len(shape) - axis_at - 1))

    gain = one(*pieces[0])
    for cut in pieces[1:]:
        gain = gain * one(*cut)
    return gain


def assign_block(own_key, own, number, rows, count, top, reach, lean):
    ranking = jax.random.permutation(own_key, count)
    crowded, ordinary = portions_of(count, rows * top, reach, lean, True), portions_of(count, rows * top, reach, lean, False)
    places = jnp.arange(count)

    def named(sizes, offset_by):
        used = int((sizes > 0).sum())
        fixed = max(1, used // 4)
        passed = fixed + (places - fixed + offset_by * (used - fixed)) % max(1, count - fixed)
        return jnp.zeros((count,), jnp.int32).at[ranking[jnp.where(places < fixed, places, passed)]].set(jnp.asarray(sizes, jnp.int32))

    sizes = jnp.where(number % 4 == 0, named(crowded, number // 4), named(ordinary, number - number // 4 - 1))
    mixed = jax.random.permutation(jax.random.fold_in(own, 3), count)
    giver, sink = mixed[0:count // 2 * 2:2], mixed[1:count // 2 * 2:2]
    slack = jnp.minimum(sizes[giver] - 1, reach - sizes[sink]) // 2
    slack = jnp.where((giver == ranking[0]) | (sink == ranking[0]) | (sizes[sink] == 0), 0, jnp.maximum(slack, 0))
    passed = jax.random.randint(jax.random.fold_in(own, 4), (count // 2,), 0, 1 << 20) % (slack + 1)
    sizes = sizes.at[giver].add(-passed).at[sink].add(passed)
    items = jnp.searchsorted(jnp.cumsum(sizes), jnp.arange(rows * top), side="right").astype(jnp.int32)
    listing = items.reshape(top, rows).T
    listing = listing[jax.random.permutation(jax.random.fold_in(own, 1), rows)]
    offset_by = jax.random.randint(jax.random.fold_in(own, 2), (rows, 1), 0, top)
    return jnp.take_along_axis(listing, (jnp.arange(top)[None, :] + offset_by) % top, axis=1)


def portions_of(amount, total, reach, slope, full):
    portions = [(1 << 20) // math.isqrt(rank ** slope) + 1 for rank in range(1, amount + 1)]
    largest = reach if full else min(reach, max(-(-total // amount), total * portions[0] // sum(portions)))
    least = 1 if total - largest >= amount - 1 else 0
    counts, spare = [largest] + [least] * (amount - 1), total - largest - least * (amount - 1)
    while spare > 0:
        free = [i for i in range(1, amount) if counts[i] < largest] or [i for i in range(1, amount) if counts[i] < reach]
        pool, remaining = sum([portions[i] for i in free]), spare
        for i in free:
            addition = min(reach - counts[i], max(1, remaining * portions[i] // pool), spare)
            counts[i] = counts[i] + addition
            spare = spare - addition
    return np.array(counts)


def noise(key, shape, scale, reach, pieces=(), kind=jnp.bfloat16):
    drawn = scale * jax.random.normal(key, shape, jnp.float32)
    if pieces:
        drawn = drawn * shard_levels(key, shape, pieces, -0.22, 0.18)
    return jnp.clip(drawn, -reach, reach).astype(kind)


def setup_inputs(seed: int = 0) -> dict:
    keys = jax.random.split(jax.random.key(seed), 6)
    panels = noise(keys[0], (2 * CH, BLOCKS * ORDER), (BLOCKS * ORDER) ** -0.5, 0.1875, ((1, 4),), jnp.float32)
    block_phase = place_ends(jax.random.randint(keys[1], (2, BLOCKS), 0, PHASEQ), jax.random.fold_in(keys[1], 1), 0, PHASEQ - 1).astype(jnp.int32)
    target_owner_keys = jax.random.split(jax.random.fold_in(keys[2], 1), TARGETS // TGT_DEV)
    target_owner_turns = jax.random.permutation(jax.random.fold_in(keys[2], 3), TARGETS // TGT_DEV)
    target_owner = jax.vmap(lambda own, number: assign_block(jax.random.fold_in(keys[2], 2), own, number, TGT_DEV, DEVICES, 1, CAP, 2))(target_owner_keys, target_owner_turns).reshape((TARGETS, 1))
    target_cell = place_ends(jax.random.randint(keys[3], (TARGETS,), 0, GS), jax.random.fold_in(keys[3], 1), 0, GS - 1).astype(jnp.int32)
    target_offset = place_ends(jax.random.randint(keys[4], (TARGETS,), 0, OFFQ), jax.random.fold_in(keys[4], 1), 0, OFFQ - 1).astype(jnp.int32)
    return dict(panels=panels, block_phase=block_phase, target_owner=target_owner, target_cell=target_cell, target_offset=target_offset)


def chebyshev(xpos, order):
    rows = [jnp.ones_like(xpos), xpos]
    for j in range(2, order):
        rows.append(2.0 * xpos * rows[-1] - rows[-2])
    return jnp.stack(rows[:order], 0)


def block_turns(phases, gpos):
    wrapped = gpos % PHASEQ
    g_high = wrapped // ROOTQ
    g_low = wrapped % ROOTQ
    p_high = phases[1] // ROOTQ
    p_low = phases[1] % ROOTQ
    cross = (g_high[None, :] * p_low[:, None] + g_low[None, :] * p_high[:, None]) % ROOTQ
    total = phases[0][:, None] + cross * ROOTQ + g_low[None, :] * p_low[:, None]
    return (total % PHASEQ).astype(jnp.int32)


def grid_terms(coeffs, phases, gpos):
    nblk = phases.shape[1]
    order = coeffs.shape[1] // nblk
    half = coeffs.shape[0] // 2
    width = gpos.shape[0]
    local = gpos - (gpos // GS) * GS
    xpos = (2 * local + 1).astype(jnp.float32) / GS - 1.0
    cheb = chebyshev(xpos, order)
    turns = block_turns(phases, gpos)
    angle = turns.astype(jnp.float32) * (2.0 * math.pi / PHASEQ)
    basis_cos = (jnp.cos(angle)[:, None, :] * cheb[None, :, :]).reshape(nblk * order, width)
    basis_sin = (jnp.sin(angle)[:, None, :] * cheb[None, :, :]).reshape(nblk * order, width)
    with_cos = jnp.dot(coeffs, basis_cos, precision=lax.Precision.HIGHEST, preferred_element_type=jnp.float32)
    with_sin = jnp.dot(coeffs, basis_sin, precision=lax.Precision.HIGHEST, preferred_element_type=jnp.float32)
    real_part = with_cos[:half] - with_sin[half:]
    imag_part = with_sin[:half] + with_cos[half:]
    return jnp.concatenate([real_part, imag_part], 0)


def kernel_rows(offsets):
    frac = (offsets.astype(jnp.float32) + 0.5) / OFFQ
    place = jnp.arange(TAPS, dtype=jnp.int32)
    dist = (place - TAPS // 2 + 1).astype(jnp.float32)[None, :] - frac[:, None]
    parity = jnp.where(place % 2 == 0, 1.0, -1.0).astype(jnp.float32)
    return parity[None, :] * jnp.sin(math.pi * frac)[:, None] / (math.pi * dist) * jnp.exp(-18.0 * dist * dist / (TAPS * TAPS))


def reference(panels, block_phase, target_owner, target_cell, target_offset):
    slabs_count = NGRID // GS
    channels = panels.shape[0]

    def one_slab(index):
        gpos = index * GS + jnp.arange(GS, dtype=jnp.int32)
        return grid_terms(panels, block_phase, gpos)

    slabs = lax.map(one_slab, jnp.arange(slabs_count, dtype=jnp.int32))
    grid_values = jnp.transpose(slabs, (1, 0, 2)).reshape(channels, NGRID)
    padded = jnp.pad(grid_values, ((0, 0), (TAPS // 2, TAPS // 2)))
    owners = target_owner[:, 0].reshape(slabs_count, TGT_DEV)
    cells = target_cell.reshape(slabs_count, TGT_DEV)
    offsets = target_offset.reshape(slabs_count, TGT_DEV)

    def one_list(items):
        owner_ids, cell_ids, offset_ids = items
        starts = (owner_ids * GS + cell_ids + 1).astype(jnp.int32)
        windows = jax.vmap(lambda begin: lax.dynamic_slice_in_dim(padded, begin, TAPS, 1))(starts)
        kernel = kernel_rows(offset_ids)
        return jnp.einsum("bct,bt->cb", windows, kernel, precision=lax.Precision.HIGHEST)

    values = lax.map(one_list, (owners, cells, offsets))
    target_values = jnp.transpose(values, (1, 0, 2)).reshape(channels, TARGETS)
    return grid_values, target_values
```

```python
import functools
import math

import jax
import jax.numpy as jnp
import ml_dtypes
import numpy as np
from jax import lax
from jax.experimental import pallas as pl
from jax.experimental.pallas import tpu as pltpu
from jax.sharding import PartitionSpec as P

TAPS = 256
OFFQ = 256
GS = 6144
PHASEQ = 4194304
TILE = 1024
TILES = GS // TILE
LANES = 256
MESH = pl.DeviceIdType.MESH
F32 = jnp.float32
BF16 = jnp.bfloat16
F8 = jnp.float8_e4m3fn
WAVE = 256.0
TAP = 256.0
SHIFTED = 64.0
PANEL = 256.0
FINE = 256.0


def local_expansion(centers, half, order):
    nodes = np.cos((np.arange(order) + 0.5) * np.pi / order)
    back = np.cos(np.outer(np.arange(order), np.arccos(nodes))) * 2.0 / order
    back[0] *= 0.5
    x = np.asarray(centers, np.float64)[:, None] + half * nodes[None, :]
    tj = np.polynomial.chebyshev.chebvander(x, order - 1)
    return np.einsum("tnj,kn->tjk", tj, back)


def split_np(x):
    hi = x.astype(np.float32).astype(ml_dtypes.bfloat16)
    lo = (x - hi.astype(np.float64)).astype(np.float32).astype(ml_dtypes.bfloat16)
    return hi, lo


def tables(order, nblk):
    half = TILE / GS
    centers = (2.0 * TILE * np.arange(TILES) + TILE) / GS - 1.0
    m = local_expansion(centers, half, order)
    gain = 400.0 / (math.sqrt(2.0) * np.abs(m).sum(1).max())
    eye = np.eye(nblk)
    big = np.einsum("tjk,bc->tbjkc", m * gain, eye).reshape(TILES, order * nblk, order * nblk)
    frac = (np.arange(OFFQ) + 0.5) / OFFQ
    place = np.arange(TAPS)
    dist = (place - TAPS // 2 + 1.0)[:, None] - frac[None, :]
    sign = np.where(place % 2 == 0, 1.0, -1.0)[:, None]
    taps = sign * np.sin(np.pi * frac)[None, :] / (np.pi * dist) * np.exp(-18.0 * dist * dist / (TAPS * TAPS))
    return split_np(big), gain, np.concatenate(split_np(taps * TAP), 0)


def split(x):
    hi = x.astype(BF16)
    return hi, x - hi.astype(F32)


def dot(a, b):
    return jnp.dot(a, b, preferred_element_type=F32)


def sincos(turns):
    turns = turns & (PHASEQ - 1)
    quad = (turns + PHASEQ // 8) >> 20
    r = (turns - (quad << 20)).astype(F32) * (2.0 * math.pi / PHASEQ)
    r2 = r * r
    s = r + r * r2 * (-1 / 6 + r2 * (1 / 120 + r2 * (-1 / 5040 + r2 * (1 / 362880))))
    c = 1.0 + r2 * (-0.5 + r2 * (1 / 24 + r2 * (-1 / 720 + r2 * (1 / 40320))))
    odd = (quad & 1) == 1
    sn = jnp.where(odd, c, s)
    cs = jnp.where(odd, s, c)
    sn = jnp.where((quad & 2) == 2, -sn, sn)
    cs = jnp.where(((quad + 1) & 2) == 2, -cs, cs)
    return sn, cs


def spread_phases(n, order, nblk, ph_ref, col_ref, row_ref):
    cols = order * nblk
    pick = (
        lax.broadcasted_iota(jnp.int32, (nblk, cols), 1) % nblk
        == lax.broadcasted_iota(jnp.int32, (nblk, cols), 0)
    ).astype(F32).astype(BF16)
    eye = (
        lax.broadcasted_iota(jnp.int32, (n * nblk, nblk), 0) % nblk
        == lax.broadcasted_iota(jnp.int32, (n * nblk, nblk), 1)
    ).astype(F32).astype(BF16)
    v = jnp.concatenate([ph_ref[i] for i in range(n)], 0)
    row = col = 0.0
    for a, part in enumerate((v & 255, (v >> 8) & 255, v >> 16)):
        part = part.astype(F32).astype(BF16)
        row += dot(part, pick) * float(256**a)
        col += lax.dot_general(eye, part, (((1,), (1,)), ((), ())), preferred_element_type=F32) * float(256**a)
    row_ref[...] = row.astype(jnp.int32)
    col = col.astype(jnp.int32)
    for i in range(n):
        rr = slice(i * nblk, (i + 1) * nblk)
        col_ref[i, :, 0:128] = jnp.broadcast_to(col[rr, 2 * i : 2 * i + 1], (nblk, 128))
        col_ref[i, :, 128:256] = jnp.broadcast_to(col[rr, 2 * i + 1 : 2 * i + 2], (nblk, 128))


def wide(x, width):
    return jnp.concatenate([x] * (width // 128), 1)


def taper_targets(n_dev, order, own_ref, cell_ref, off_ref, tap_ref, kern_ref, th, t8):
    count = own_ref.shape[1]
    hot = (lax.broadcasted_iota(jnp.int32, (OFFQ, count), 0) == off_ref[...]).astype(F32).astype(BF16)
    kern = dot(tap_ref[...], hot)
    kern_ref[...] = kern[:TAPS] + kern[TAPS:]

    def rows(r, carry):
        at = pl.multiple_of(r * 32, 32)
        low = pl.multiple_of(TAPS + r * 32, 32)
        for l0 in range(0, count, LANES):
            ll = slice(l0, l0 + LANES)
            owner = own_ref[:, ll]
            first = jnp.where(owner == 0, 0, -GS)
            last = jnp.where(owner == n_dev - 1, GS, 2 * GS)
            pos = lax.broadcasted_iota(jnp.int32, (32, LANES), 0) + (cell_ref[:, ll] + (at - (TAPS // 2 - 1)))
            valid = (pos >= first) & (pos < last)
            m = jnp.where(pos < 0, pos + GS, pos)
            m = jnp.where(m >= GS, m - GS, m)
            x = (2 * m + 1).astype(F32) * (1.0 / GS) - 1.0
            before = jnp.where(valid, kern_ref[pl.ds(at, 32), ll], 0.0)
            now = x * before
            x2 = x + x
            for j in range(order):
                hi, lo = split(before)
                th[j, pl.ds(at, 32), ll] = hi
                t8[j, pl.ds(at, 32), ll] = hi.astype(F8)
                t8[j, pl.ds(low, 32), ll] = lo.astype(F8)
                before, now = now, x2 * now - before
        return carry

    lax.fori_loop(0, TAPS // 32, rows, 0)


def fill_basis(n, order, nblk, col_ref, bh, b8h, b8l):
    def chunk(i, carry):
        for l0 in range(0, TILE, LANES):
            lane = lax.broadcasted_iota(jnp.int32, (nblk, LANES), 1) + l0
            sn, cs = sincos(lane * wide(col_ref[i, :, 128:256], LANES))
            y = (2 * lane + 1).astype(F32) * (1.0 / TILE) - 1.0
            y2 = y + y
            waves = (cs * WAVE, sn * WAVE)
            before, now = jnp.ones_like(y), y
            for k in range(0, order, 2):
                at = pl.multiple_of(i * order * nblk + k * nblk, 32)
                for part, wave in enumerate(waves):
                    ll = slice(part * TILE + l0, part * TILE + l0 + LANES)
                    hi, lo = split(jnp.concatenate([wave * before, wave * now], 0))
                    bh[pl.ds(at, 2 * nblk), ll] = hi
                    b8h[pl.ds(at, 2 * nblk), ll] = hi.astype(F8)
                    b8l[pl.ds(at, 2 * nblk), ll] = lo.astype(F8)
                before = y2 * now - before
                now = y2 * before - now
        return carry

    lax.fori_loop(0, n, chunk, 0)


def fill_waves(n, nblk, col_ref, eh, e8):
    lane = lax.broadcasted_iota(jnp.int32, (nblk, TAPS), 1)

    def chunk(i, carry):
        sn, cs = sincos(lane * wide(col_ref[i, :, 128:256], TAPS))
        at = pl.multiple_of(i * 2 * nblk, 2 * nblk)
        hi, lo = split(jnp.concatenate([cs, sn], 0) * WAVE)
        eh[pl.ds(at, 2 * nblk), :] = hi
        e8[pl.ds(at, 2 * nblk), 0:TAPS] = lo.astype(F8)
        e8[pl.ds(at, 2 * nblk), TAPS : 2 * TAPS] = hi.astype(F8)
        return carry

    lax.fori_loop(0, n, chunk, 0)


def prepare_kernel(
    n, n_dev, order, nblk,
    pan_hbm, ph_hbm, own_hbm, cell_hbm, off_hbm, tap_hbm, mh_hbm, ml_hbm,
    pan_ref, row_ref, bh, b8h, b8l, vh, v8h, v8l, m_ref,
    ph_ref, own_ref, cell_ref, off_ref, tap_ref,
    load_sem, own_sem, send_sem, recv_sem, pass_sem, got_sem,
    col_ref, kern_ref, th, t8, eh, e8, c1, s1,
):
    cols = order * nblk
    rows = pan_ref.shape[1]
    half = rows // 2
    count = own_ref.shape[1]
    me = lax.axis_index("term")
    slab = lax.axis_index("slab")
    core = lax.rem(slab, 2)
    twin = {"slab": slab + 1 - 2 * core}
    mine = pl.ds(pl.multiple_of(core * half, half), half)
    barrier = pltpu.get_barrier_semaphore()
    for d in range(1, n):
        pl.semaphore_signal(barrier, inc=1, device_id={"term": lax.rem(me + d, n)}, device_id_type=MESH)
    pl.semaphore_signal(barrier, inc=1, device_id=twin, device_id_type=MESH)
    loads = [
        pltpu.make_async_copy(src, dst, load_sem.at[a])
        for a, (src, dst) in enumerate(
            (
                (own_hbm, own_ref), (cell_hbm, cell_ref), (off_hbm, off_ref), (tap_hbm, tap_ref),
                (mh_hbm, m_ref.at[0]), (ml_hbm, m_ref.at[1]),
            )
        )
    ]
    for copy in loads:
        copy.start()
    owned = [
        pltpu.make_async_copy(src, dst.at[me], own_sem.at[a])
        for a, (src, dst) in enumerate(((pan_hbm, pan_ref), (ph_hbm, ph_ref)))
    ]
    for copy in owned:
        copy.start()
    pl.semaphore_wait(barrier, n)
    bigs, smalls = [], []
    for d in sorted(range(1, n), key=lambda d: -min(d, n - d)):
        peer = {"term": lax.rem(me + d, n)}
        smalls.append(
            pltpu.make_async_remote_copy(
                src_ref=ph_hbm, dst_ref=ph_ref.at[me], send_sem=send_sem.at[1, d], recv_sem=recv_sem.at[1, d],
                device_id=peer, device_id_type=MESH,
            )
        )
        bigs.append((
            d,
            pltpu.make_async_remote_copy(
                src_ref=pan_hbm.at[mine], dst_ref=pan_ref.at[me, mine], send_sem=send_sem.at[0, d],
                recv_sem=recv_sem.at[0, d], device_id=peer, device_id_type=MESH,
            ),
        ))
    for small in smalls:
        small.start()
    for _, big in bigs:
        big.start()
    for copy in loads[:4]:
        copy.wait()
    taper_targets(n_dev, order, own_ref, cell_ref, off_ref, tap_ref, kern_ref, th, t8)
    owned[1].wait()
    for small in smalls:
        small.wait()
    spread_phases(n, order, nblk, ph_ref, col_ref, row_ref)
    passes = []
    for d, big in reversed(bigs):
        big.wait_recv()
        origin = lax.rem(me - d + n, n)
        passed = pltpu.make_async_remote_copy(
            src_ref=pan_ref.at[origin, mine], dst_ref=pan_ref.at[origin, mine],
            send_sem=pass_sem.at[d], recv_sem=got_sem.at[d], device_id=twin, device_id_type=MESH,
        )
        passed.start()
        passes.append(passed)
    fill_basis(n, order, nblk, col_ref, bh, b8h, b8l)
    fill_waves(n, nblk, col_ref, eh, e8)

    first = own_ref[...] * GS + cell_ref[...] - (TAPS // 2 - 1)

    def first_phase(i, carry):
        sn, cs = sincos(wide(col_ref[i, :, 0:128], count) + first * wide(col_ref[i, :, 128:256], count))
        at = pl.multiple_of(i * nblk, nblk)
        c1[pl.ds(at, nblk), :] = cs * (SHIFTED / (WAVE * TAP))
        s1[pl.ds(at, nblk), :] = sn * (SHIFTED / (WAVE * TAP))
        return carry

    lax.fori_loop(0, n, first_phase, 0)

    def moments(j2, carry):
        v = [
            dot(eh[...], th[2 * j2 + a]) + dot(e8[...], t8[2 * j2 + a])
            for a in range(2)
        ]
        for i in range(n):
            at = pl.multiple_of(i * cols + j2 * 2 * nblk, 2 * nblk)
            for l0 in range(0, count, LANES):
                ll = slice(l0, l0 + LANES)
                cs = c1[i * nblk : (i + 1) * nblk, ll]
                sn = s1[i * nblk : (i + 1) * nblk, ll]
                vc = [u[i * 2 * nblk : i * 2 * nblk + nblk, ll] for u in v]
                vs = [u[i * 2 * nblk + nblk : (i + 1) * 2 * nblk, ll] for u in v]
                re = jnp.concatenate([cs * a - sn * b for a, b in zip(vc, vs)], 0)
                im = jnp.concatenate([sn * a + cs * b for a, b in zip(vc, vs)], 0)
                for part, w in enumerate((re, im)):
                    lp = slice(part * count + l0, part * count + l0 + LANES)
                    hi, lo = split(w)
                    vh[pl.ds(at, 2 * nblk), lp] = hi
                    v8h[pl.ds(at, 2 * nblk), lp] = hi.astype(F8)
                    v8l[pl.ds(at, 2 * nblk), lp] = lo.astype(F8)
        return carry

    lax.fori_loop(0, order // 2, moments, 0)

    for copy in loads[4:]:
        copy.wait()
    owned[0].wait()
    for passed in passes:
        passed.wait()
    for _, big in bigs:
        big.wait_send()


def product_kernel(
    n, order, nblk, gain,
    pan_ref, row_ref, bh, b8h, b8l, vh, v8h, v8l, m_ref,
    grid_out, val_ref,
    store_sem, grid_ref, ah, a8h, a8l, ph, p8h, p8l,
):
    cols = order * nblk
    rows = pan_ref.shape[1]
    half = rows // 2
    count = vh.shape[1] // 2
    r = lax.broadcasted_iota(jnp.int32, (cols, cols), 0)
    c = lax.broadcasted_iota(jnp.int32, (cols, cols), 1)
    perm = ((r % order == c // nblk) & (r // order == c % nblk)).astype(F32).astype(BF16)
    base = (lax.axis_index("slab") * n + lax.axis_index("term")) * GS
    top = jnp.max(jnp.abs(pan_ref[0]))
    for i in range(1, n):
        top = jnp.maximum(top, jnp.max(jnp.abs(pan_ref[i])))
    top = jnp.maximum(top, 1e-30)
    scale = PANEL / jnp.full((8, 128), top, F32)
    unscale = jnp.full((8, 128), top, F32) * (1.0 / PANEL)
    scale = jnp.concatenate([wide(scale, cols)] * (rows // 8), 0)
    spin = lax.broadcasted_iota(jnp.int32, (8, cols), 0) * TILE + base

    def grid_chunk(i, carry):
        ps_h, ps_l = split(pan_ref[i] * scale)
        both = jnp.concatenate([ps_h, ps_l.astype(BF16)], 0)
        at = pl.ds(pl.multiple_of(i * cols, cols), cols)
        pp = dot(both, perm)
        pph = pp[:rows].astype(BF16)
        ph[:, at] = pph
        p8h[:, at] = pph.astype(F8)
        p8l[:, at] = (pp[rows:] * FINE).astype(F8)
        sn, cs = sincos(row_ref[pl.ds(2 * i, 1), :] + spin * row_ref[pl.ds(2 * i + 1, 1), :])
        sn, cs = sn * (1.0 / PANEL), cs * (1.0 / PANEL)
        for t in range(TILES):
            z2 = dot(both, m_ref[0, t])
            z = z2[:rows] + z2[rows:] + dot(ps_h, m_ref[1, t])
            zr, zi = z[:half], z[half:]
            ct, st = cs[t : t + 1], sn[t : t + 1]
            q = jnp.concatenate([ct * zr - st * zi, ct * zi + st * zr], 0)
            hi, lo = split(q)
            rr = slice(t * rows, (t + 1) * rows)
            ah[rr, at] = hi
            a8h[rr, at] = hi.astype(F8)
            a8l[rr, at] = (lo * FINE).astype(F8)
        return carry

    lax.fori_loop(0, n, grid_chunk, 0)

    down = wide(unscale, LANES) * (PANEL / (WAVE * gain))
    down = jnp.concatenate([down] * (half // 8), 0)
    for lo_col in range(0, TILE, LANES):
        acc = []
        for part in range(2):
            cc = slice(part * TILE + lo_col, part * TILE + lo_col + LANES)
            x = dot(ah[...], bh[:, cc]) + dot(a8h[...], b8l[:, cc])
            acc.append(x + dot(a8l[...], b8h[:, cc]) * (1.0 / FINE))
        for t in range(TILES):
            cc = slice(t * TILE + lo_col, t * TILE + lo_col + LANES)
            a, b = t * rows, t * rows + half
            grid_ref[:half, cc] = (acc[0][a:b] - acc[1][b : b + half]) * down
            grid_ref[half:, cc] = (acc[0][b : b + half] + acc[1][a:b]) * down

    store = pltpu.make_async_copy(grid_ref, grid_out, store_sem)
    store.start()
    down = wide(unscale, count) * (1.0 / SHIFTED)
    down = jnp.concatenate([down] * (half // 8), 0)
    x = dot(ph[...], vh[...]) + dot(p8h[...], v8l[...]) + dot(p8l[...], v8h[...]) * (1.0 / FINE)
    val_ref[:half] = (x[:half, :count] - x[half:, count:]) * down
    val_ref[half:] = (x[half:, :count] + x[:half, count:]) * down
    store.wait()


def in_hbm(x):
    return pltpu.with_memory_space_constraint(x, pltpu.HBM)


def body(n_slab, n, panels, block_phase, target_owner, target_cell, target_offset):
    n_dev = n_slab * n
    channels = panels.shape[0]
    nblk = block_phase.shape[1]
    order = panels.shape[1] // nblk
    cols = order * nblk
    targets = target_cell.shape[0]
    (mh, ml), gain, taps = tables(order, nblk)
    vmem = pl.BlockSpec(memory_space=pltpu.VMEM)
    hbm = pl.BlockSpec(memory_space=pl.ANY)
    deep = n * cols
    ready = pl.pallas_call(
        functools.partial(prepare_kernel, n, n_dev, order, nblk),
        out_shape=(
            pltpu.VMEM((n, channels, cols), F32),
            pltpu.VMEM((2 * n, cols), jnp.int32),
            pltpu.VMEM((deep, 2 * TILE), BF16),
            pltpu.VMEM((deep, 2 * TILE), F8),
            pltpu.VMEM((deep, 2 * TILE), F8),
            pltpu.VMEM((deep, 2 * targets), BF16),
            pltpu.VMEM((deep, 2 * targets), F8),
            pltpu.VMEM((deep, 2 * targets), F8),
            pltpu.VMEM((2, TILES, cols, cols), BF16),
        ),
        in_specs=[hbm] * 8,
        out_specs=(vmem,) * 9,
        scratch_shapes=[
            pltpu.VMEM((n, 2, nblk), jnp.int32),
            pltpu.VMEM((1, targets), jnp.int32),
            pltpu.VMEM((1, targets), jnp.int32),
            pltpu.VMEM((1, targets), jnp.int32),
            pltpu.VMEM((2 * TAPS, OFFQ), BF16),
            pltpu.SemaphoreType.DMA((6,)),
            pltpu.SemaphoreType.DMA((2,)),
            pltpu.SemaphoreType.DMA((2, n)),
            pltpu.SemaphoreType.DMA((2, n)),
            pltpu.SemaphoreType.DMA((n,)),
            pltpu.SemaphoreType.DMA((n,)),
            pltpu.VMEM((n, nblk, 256), jnp.int32),
            pltpu.VMEM((TAPS, targets), F32),
            pltpu.VMEM((order, TAPS, targets), BF16),
            pltpu.VMEM((order, 2 * TAPS, targets), F8),
            pltpu.VMEM((n * 2 * nblk, TAPS), BF16),
            pltpu.VMEM((n * 2 * nblk, 2 * TAPS), F8),
            pltpu.VMEM((n * nblk, targets), F32),
            pltpu.VMEM((n * nblk, targets), F32),
        ],
        compiler_params=pltpu.CompilerParams(
            collective_id=0, has_side_effects=True, vmem_limit_bytes=20 << 20
        ),
    )(
        *map(
            in_hbm,
            (
                panels,
                block_phase,
                target_owner.reshape(1, targets),
                target_cell.reshape(1, targets),
                target_offset.reshape(1, targets),
                jnp.asarray(taps),
                jnp.asarray(mh),
                jnp.asarray(ml),
            ),
        )
    )
    return pl.pallas_call(
        functools.partial(product_kernel, n, order, nblk, gain),
        out_shape=(
            jax.ShapeDtypeStruct((channels, GS), F32),
            jax.ShapeDtypeStruct((channels, targets), F32),
        ),
        in_specs=[vmem] * 9,
        out_specs=(hbm, vmem),
        scratch_shapes=[
            pltpu.SemaphoreType.DMA,
            pltpu.VMEM((channels, GS), F32),
            pltpu.VMEM((TILES * channels, deep), BF16),
            pltpu.VMEM((TILES * channels, deep), F8),
            pltpu.VMEM((TILES * channels, deep), F8),
            pltpu.VMEM((channels, deep), BF16),
            pltpu.VMEM((channels, deep), F8),
            pltpu.VMEM((channels, deep), F8),
        ],
        compiler_params=pltpu.CompilerParams(vmem_limit_bytes=24 << 20),
    )(*ready)


def solution(mesh):
    placed = (
        P(None, "term"),
        P(None, "term"),
        P(("slab", "term"), None),
        P(("slab", "term")),
        P(("slab", "term")),
    )
    return jax.shard_map(
        functools.partial(body, mesh.shape["slab"], mesh.shape["term"]),
        mesh=mesh,
        in_specs=placed,
        out_specs=(P(None, ("slab", "term")), P(None, ("slab", "term"))),
        check_vma=False,
    )
```

```python
import functools
import math

import jax
import jax.numpy as jnp
import ml_dtypes
import numpy as np
from jax import lax
from jax.experimental import pallas as pl
from jax.experimental.pallas import tpu as pltpu
from jax.sharding import PartitionSpec as P

TAPS = 256
OFFQ = 256
GS = 6144
PHASEQ = 4194304
TILE = 1024
TILES = GS // TILE
LANES = 256
MESH = pl.DeviceIdType.MESH
F32 = jnp.float32
BF16 = jnp.bfloat16
F8 = jnp.float8_e4m3fn
WAVE = 256.0
TAP = 256.0
SHIFTED = 64.0
PANEL = 256.0
FINE = 256.0


def local_expansion(centers, half, order):
    nodes = np.cos((np.arange(order) + 0.5) * np.pi / order)
    back = np.cos(np.outer(np.arange(order), np.arccos(nodes))) * 2.0 / order
    back[0] *= 0.5
    x = np.asarray(centers, np.float64)[:, None] + half * nodes[None, :]
    tj = np.polynomial.chebyshev.chebvander(x, order - 1)
    return np.einsum("tnj,kn->tjk", tj, back)


def split_np(x):
    hi = x.astype(np.float32).astype(ml_dtypes.bfloat16)
    lo = (x - hi.astype(np.float64)).astype(np.float32).astype(ml_dtypes.bfloat16)
    return hi, lo


def tables(order, nblk):
    half = TILE / GS
    centers = (2.0 * TILE * np.arange(TILES) + TILE) / GS - 1.0
    m = local_expansion(centers, half, order)
    gain = 400.0 / (math.sqrt(2.0) * np.abs(m).sum(1).max())
    eye = np.eye(nblk)
    big = np.einsum("tjk,bc->tbjkc", m * gain, eye).reshape(TILES, order * nblk, order * nblk)
    frac = (np.arange(OFFQ) + 0.5) / OFFQ
    place = np.arange(TAPS)
    dist = (place - TAPS // 2 + 1.0)[:, None] - frac[None, :]
    sign = np.where(place % 2 == 0, 1.0, -1.0)[:, None]
    taps = sign * np.sin(np.pi * frac)[None, :] / (np.pi * dist) * np.exp(-18.0 * dist * dist / (TAPS * TAPS))
    return split_np(big), gain, np.concatenate(split_np(taps * TAP), 0)


def split(x):
    hi = x.astype(BF16)
    return hi, x - hi.astype(F32)


def dot(a, b):
    return jnp.dot(a, b, preferred_element_type=F32)


def sincos(turns):
    turns = turns & (PHASEQ - 1)
    quad = (turns + PHASEQ // 8) >> 20
    r = (turns - (quad << 20)).astype(F32) * (2.0 * math.pi / PHASEQ)
    r2 = r * r
    s = r + r * r2 * (-1 / 6 + r2 * (1 / 120 + r2 * (-1 / 5040 + r2 * (1 / 362880))))
    c = 1.0 + r2 * (-0.5 + r2 * (1 / 24 + r2 * (-1 / 720 + r2 * (1 / 40320))))
    odd = (quad & 1) == 1
    sn = jnp.where(odd, c, s)
    cs = jnp.where(odd, s, c)
    sn = jnp.where((quad & 2) == 2, -sn, sn)
    cs = jnp.where(((quad + 1) & 2) == 2, -cs, cs)
    return sn, cs


def spread_phases(order, nblk, chunks, ph_ref, col_ref, row_ref):
    cols = order * nblk
    many = 2 * len(chunks)
    r = lax.broadcasted_iota(jnp.int32, (3 * nblk, cols), 0)
    c = lax.broadcasted_iota(jnp.int32, (3 * nblk, cols), 1)
    size = jnp.where(r < nblk, 1.0, jnp.where(r < 2 * nblk, 256.0, 65536.0))
    pick = jnp.where(c % nblk == r % nblk, size, 0.0).astype(BF16)
    r = lax.broadcasted_iota(jnp.int32, (nblk, 3 * nblk), 0)
    c = lax.broadcasted_iota(jnp.int32, (nblk, 3 * nblk), 1)
    size = jnp.where(c < nblk, 1.0, jnp.where(c < 2 * nblk, 256.0, 65536.0))
    eye = jnp.where(c % nblk == r, size, 0.0).astype(BF16)
    v = jnp.concatenate([ph_ref[i] for i in chunks] + [jnp.zeros((-many % 16, nblk), jnp.int32)], 0)
    parts = jnp.concatenate([(v & 255).astype(F32), ((v >> 8) & 255).astype(F32), (v >> 16).astype(F32)], 1)
    parts = parts.astype(BF16)
    row = dot(parts, pick).astype(jnp.int32)
    col = lax.dot_general(eye, parts, (((1,), (1,)), ((), ())), preferred_element_type=F32).astype(jnp.int32)
    for a, i in enumerate(chunks):
        row_ref[i] = row[2 * a : 2 * a + 2]
        col_ref[i, :, 0:128] = jnp.broadcast_to(col[:, 2 * a : 2 * a + 1], (nblk, 128))
        col_ref[i, :, 128:256] = jnp.broadcast_to(col[:, 2 * a + 1 : 2 * a + 2], (nblk, 128))


def wide(x, width):
    return jnp.concatenate([x] * (width // 128), 1)


def taper_targets(n_dev, order, own_ref, cell_ref, off_ref, tap_ref, kern_ref, th, t8):
    count = own_ref.shape[1]
    hot = (lax.broadcasted_iota(jnp.int32, (OFFQ, count), 0) == off_ref[...]).astype(F32).astype(BF16)
    kern = dot(tap_ref[...], hot)
    kern_ref[...] = kern[:TAPS] + kern[TAPS:]

    def rows(r, carry):
        at = pl.multiple_of(r * 32, 32)
        low = pl.multiple_of(TAPS + r * 32, 32)
        for l0 in range(0, count, LANES):
            ll = slice(l0, l0 + LANES)
            owner = own_ref[:, ll]
            first = jnp.where(owner == 0, 0, -GS)
            last = jnp.where(owner == n_dev - 1, GS, 2 * GS)
            pos = lax.broadcasted_iota(jnp.int32, (32, LANES), 0) + (cell_ref[:, ll] + (at - (TAPS // 2 - 1)))
            valid = (pos >= first) & (pos < last)
            m = jnp.where(pos < 0, pos + GS, pos)
            m = jnp.where(m >= GS, m - GS, m)
            x = (2 * m + 1).astype(F32) * (1.0 / GS) - 1.0
            before = jnp.where(valid, kern_ref[pl.ds(at, 32), ll], 0.0)
            now = x * before
            x2 = x + x
            for j in range(order):
                hi, lo = split(before)
                th[j, pl.ds(at, 32), ll] = hi
                t8[j, pl.ds(at, 32), ll] = hi.astype(F8)
                t8[j, pl.ds(low, 32), ll] = lo.astype(F8)
                before, now = now, x2 * now - before
        return carry

    return rows


def fill_basis(order, nblk, i, col_ref, bh, b8h, b8l):
    for l0 in range(0, TILE, LANES):
        lane = lax.broadcasted_iota(jnp.int32, (nblk, LANES), 1) + l0
        sn, cs = sincos(lane * wide(col_ref[i, :, 128:256], LANES))
        y = (2 * lane + 1).astype(F32) * (1.0 / TILE) - 1.0
        y2 = y + y
        waves = (cs * WAVE, sn * WAVE)
        before, now = jnp.ones_like(y), y
        for k in range(0, order, 2):
            at = pl.multiple_of(i * order * nblk + k * nblk, 32)
            for part, wave in enumerate(waves):
                ll = slice(part * TILE + l0, part * TILE + l0 + LANES)
                hi, lo = split(jnp.concatenate([wave * before, wave * now], 0))
                bh[pl.ds(at, 2 * nblk), ll] = hi
                b8h[pl.ds(at, 2 * nblk), ll] = hi.astype(F8)
                b8l[pl.ds(at, 2 * nblk), ll] = lo.astype(F8)
            before = y2 * now - before
            now = y2 * before - now


def fill_waves(nblk, i, col_ref, eh, e8):
    lane = lax.broadcasted_iota(jnp.int32, (nblk, TAPS), 1)
    sn, cs = sincos(lane * wide(col_ref[i, :, 128:256], TAPS))
    at = pl.multiple_of(i * 2 * nblk, 2 * nblk)
    hi, lo = split(jnp.concatenate([cs, sn], 0) * WAVE)
    eh[pl.ds(at, 2 * nblk), :] = hi
    e8[pl.ds(at, 2 * nblk), 0:TAPS] = lo.astype(F8)
    e8[pl.ds(at, 2 * nblk), TAPS : 2 * TAPS] = hi.astype(F8)


def first_phases(nblk, i, first, col_ref, c1, s1):
    count = first.shape[1]
    sn, cs = sincos(wide(col_ref[i, :, 0:128], count) + first * wide(col_ref[i, :, 128:256], count))
    at = pl.multiple_of(i * nblk, nblk)
    c1[pl.ds(at, nblk), :] = cs * (SHIFTED / (WAVE * TAP))
    s1[pl.ds(at, nblk), :] = sn * (SHIFTED / (WAVE * TAP))


def prepare_kernel(
    n, n_dev, order, nblk,
    pan_hbm, ph_hbm, own_hbm, cell_hbm, off_hbm, tap_hbm, mh_hbm, ml_hbm,
    pan_ref, row_ref, bh, b8h, b8l, th, t8, eh, e8, c1, s1, m_ref,
    ph_ref, own_ref, cell_ref, off_ref, tap_ref,
    load_sem, own_sem, send_sem, recv_sem, pass_sem, got_sem,
    col_ref, kern_ref,
):
    cols = order * nblk
    rows = pan_ref.shape[1]
    half = rows // 2
    count = own_ref.shape[1]
    me = lax.axis_index("term")
    slab = lax.axis_index("slab")
    core = lax.rem(slab, 2)
    twin = {"slab": slab + 1 - 2 * core}
    mine = pl.ds(pl.multiple_of(core * half, half), half)
    barrier = pltpu.get_barrier_semaphore()
    for d in range(1, n):
        pl.semaphore_signal(barrier, inc=1, device_id={"term": lax.rem(me + d, n)}, device_id_type=MESH)
    pl.semaphore_signal(barrier, inc=1, device_id=twin, device_id_type=MESH)
    loads = [
        pltpu.make_async_copy(src, dst, load_sem.at[a])
        for a, (src, dst) in enumerate(
            (
                (own_hbm, own_ref), (cell_hbm, cell_ref), (off_hbm, off_ref), (tap_hbm, tap_ref),
                (mh_hbm, m_ref.at[0]), (ml_hbm, m_ref.at[1]),
            )
        )
    ]
    for copy in loads[:4]:
        copy.start()
    owned = [
        pltpu.make_async_copy(src, dst.at[me], own_sem.at[a])
        for a, (src, dst) in enumerate(((pan_hbm, pan_ref), (ph_hbm, ph_ref)))
    ]
    for copy in owned:
        copy.start()
    for copy in loads[:4]:
        copy.wait()
    taper = taper_targets(n_dev, order, own_ref, cell_ref, off_ref, tap_ref, kern_ref, th, t8)
    pl.semaphore_wait(barrier, n)
    bigs, smalls = [], []
    for d in sorted(range(1, n), key=lambda d: -min(d, n - d)):
        peer = {"term": lax.rem(me + d, n)}
        smalls.append(
            pltpu.make_async_remote_copy(
                src_ref=ph_hbm, dst_ref=ph_ref.at[me], send_sem=send_sem.at[1, d], recv_sem=recv_sem.at[1, d],
                device_id=peer, device_id_type=MESH,
            )
        )
        bigs.append((
            d,
            pltpu.make_async_remote_copy(
                src_ref=pan_hbm.at[mine], dst_ref=pan_ref.at[me, mine], send_sem=send_sem.at[0, d],
                recv_sem=recv_sem.at[0, d], device_id=peer, device_id_type=MESH,
            ),
        ))
    for small in smalls:
        small.start()
    for _, big in bigs:
        big.start()
    for copy in loads[4:]:
        copy.start()
    lax.fori_loop(0, TAPS // 32, taper, 0)
    first = own_ref[...] * GS + cell_ref[...] - (TAPS // 2 - 1)

    def chunk(d, carry):
        i = lax.rem(me + d, n)
        fill_waves(nblk, i, col_ref, eh, e8)
        first_phases(nblk, i, first, col_ref, c1, s1)
        fill_basis(order, nblk, i, col_ref, bh, b8h, b8l)
        return carry

    owned[1].wait()
    spread_phases(order, nblk, [me], ph_ref, col_ref, row_ref)
    lax.fori_loop(0, 1, chunk, 0)
    for small in smalls:
        small.wait_recv()
    spread_phases(order, nblk, [lax.rem(me + d, n) for d in range(1, n)], ph_ref, col_ref, row_ref)
    lax.fori_loop(1, n - 1, chunk, 0)
    passes = []
    for d, big in reversed(bigs):
        big.wait_recv()
        origin = lax.rem(me - d + n, n)
        passed = pltpu.make_async_remote_copy(
            src_ref=pan_ref.at[origin, mine], dst_ref=pan_ref.at[origin, mine],
            send_sem=pass_sem.at[d], recv_sem=got_sem.at[d], device_id=twin, device_id_type=MESH,
        )
        passed.start()
        passes.append(passed)
    lax.fori_loop(n - 1, n, chunk, 0)
    for copy in loads[4:]:
        copy.wait()
    owned[0].wait()
    for passed in passes:
        passed.wait()
    for small in smalls:
        small.wait_send()
    for _, big in bigs:
        big.wait_send()


def moments(n, nblk, order, j2, th, t8, eh, e8, c1, s1, vh, v8h, v8l):
    cols = order * nblk
    count = c1.shape[1]
    for l0 in range(0, count, LANES):
        ll = slice(l0, l0 + LANES)
        v = [dot(eh[...], th[2 * j2 + a, :, ll]) + dot(e8[...], t8[2 * j2 + a, :, ll]) for a in range(2)]
        for i in range(n):
            at = slice(i * cols + j2 * 2 * nblk, i * cols + (j2 + 1) * 2 * nblk)
            cs = c1[i * nblk : (i + 1) * nblk, ll]
            sn = s1[i * nblk : (i + 1) * nblk, ll]
            vc = [u[i * 2 * nblk : i * 2 * nblk + nblk] for u in v]
            vs = [u[i * 2 * nblk + nblk : (i + 1) * 2 * nblk] for u in v]
            re = jnp.concatenate([cs * a - sn * b for a, b in zip(vc, vs)], 0)
            im = jnp.concatenate([sn * a + cs * b for a, b in zip(vc, vs)], 0)
            for part, w in enumerate((re, im)):
                lp = slice(part * count + l0, part * count + l0 + LANES)
                hi, lo = split(w)
                vh[at, lp] = hi
                v8h[at, lp] = hi.astype(F8)
                v8l[at, lp] = lo.astype(F8)


def scales(top):
    top = jnp.full((8, 128), jnp.maximum(top, 1e-30), F32)
    return 1.0 / top, top


def spread_rows(x, rows):
    return jnp.concatenate([x] * (rows // 8), 0)


def both_halves(x):
    hi, lo = split(x)
    return hi, lo.astype(BF16)


def spun(d, spin, row_ref, spin_ref):
    sn, cs = sincos(row_ref[d, 0:1, :] + spin * row_ref[d, 1:2, :])
    spin_ref[d, 0] = sn
    spin_ref[d, 1] = cs


def rotate_tile(rows, slots, t, both_ref, scale, spin_ref, m_ref, ah, a8h, a8l):
    half = rows // 2
    cols = both_ref.shape[1]
    many = len(slots) * rows
    z2 = dot(both_ref[...], m_ref[0, t])
    z2 = z2[:many] + z2[many:] + dot(both_ref[0:many, :], m_ref[1, t])
    rr = slice(t * rows, (t + 1) * rows)
    for a, d in enumerate(slots):
        z = z2[a * rows : (a + 1) * rows]
        zr, zi = z[:half], z[half:]
        by = wide(scale[0:1], cols)
        st = spin_ref[d, 0, t : t + 1, :] * by
        ct = spin_ref[d, 1, t : t + 1, :] * by
        hi, lo = split(jnp.concatenate([ct * zr - st * zi, ct * zi + st * zr], 0))
        at = slice(a * cols, (a + 1) * cols)
        ah[rr, at] = hi
        a8h[rr, at] = hi.astype(F8)
        a8l[rr, at] = (lo * FINE).astype(F8)


def product_kernel(
    n, order, nblk, gain,
    pan_ref, row_ref, bh, b8h, b8l, th, t8, eh, e8, c1, s1, m_ref,
    grid_out, val_ref,
    store_sem, grid_ref, spin_ref, both_ref, ah, a8h, a8l, ph, p8h, p8l, vh, v8h, v8l,
):
    cols = order * nblk
    rows = pan_ref.shape[1]
    half = rows // 2
    count = vh.shape[1] // 2
    r = lax.broadcasted_iota(jnp.int32, (cols, cols), 0)
    c = lax.broadcasted_iota(jnp.int32, (cols, cols), 1)
    perm = ((r % order == c // nblk) & (r // order == c % nblk)).astype(F32).astype(BF16)
    base = (lax.axis_index("slab") * n + lax.axis_index("term")) * GS
    top = jnp.max(jnp.abs(pan_ref[0]))
    for i in range(1, n):
        top = jnp.maximum(top, jnp.max(jnp.abs(pan_ref[i])))
    scale, unscale = scales(top)
    spin = lax.broadcasted_iota(jnp.int32, (8, cols), 0) * TILE + base
    for i in range(n):
        spun(i, spin, row_ref, spin_ref)
        hi, lo = both_halves(pan_ref[i])
        both_ref[i * rows : (i + 1) * rows] = hi
        both_ref[(n + i) * rows : (n + i + 1) * rows] = lo
    for t in range(TILES):
        rotate_tile(rows, list(range(n)), t, both_ref, scale, spin_ref, m_ref, ah, a8h, a8l)
    pp = dot(both_ref[...], perm)
    pp = pp[: n * rows] + pp[n * rows :]
    for i in range(n):
        hi, lo = split(pp[i * rows : (i + 1) * rows] * (spread_rows(wide(scale, cols), rows) * PANEL))
        at = slice(i * cols, (i + 1) * cols)
        ph[:, at] = hi
        p8h[:, at] = hi.astype(F8)
        p8l[:, at] = (lo * FINE).astype(F8)

    down = wide(unscale, LANES) * (1.0 / (WAVE * gain))
    down = jnp.concatenate([down] * (half // 8), 0)
    pairs = order // 2
    chunks = TILE // LANES
    stores = []
    for chunk in range(chunks):
        acc = []
        for part in range(2):
            cc = slice(part * TILE + chunk * LANES, part * TILE + (chunk + 1) * LANES)
            x = dot(ah[...], bh[:, cc]) + dot(a8h[...], b8l[:, cc])
            acc.append(x + dot(a8l[...], b8h[:, cc]) * (1.0 / FINE))
        for j2 in range(chunk * pairs // chunks, (chunk + 1) * pairs // chunks):
            moments(n, nblk, order, j2, th, t8, eh, e8, c1, s1, vh, v8h, v8l)
        for t in range(TILES):
            cc = slice(t * TILE + chunk * LANES, t * TILE + (chunk + 1) * LANES)
            a, b = t * rows, t * rows + half
            grid_ref[:half, cc] = (acc[0][a:b] - acc[1][b : b + half]) * down
            grid_ref[half:, cc] = (acc[0][b : b + half] + acc[1][a:b]) * down
            store = pltpu.make_async_copy(grid_ref.at[:, cc], grid_out.at[:, cc], store_sem.at[chunk * TILES + t])
            store.start()
            stores.append(store)

    down = wide(unscale, count) * (1.0 / (SHIFTED * PANEL))
    down = jnp.concatenate([down] * (half // 8), 0)
    x = dot(ph[...], vh[...]) + dot(p8h[...], v8l[...]) + dot(p8l[...], v8h[...]) * (1.0 / FINE)
    val_ref[:half] = (x[:half, :count] - x[half:, count:]) * down
    val_ref[half:] = (x[half:, :count] + x[:half, count:]) * down
    for store in stores:
        store.wait()


def in_hbm(x):
    return pltpu.with_memory_space_constraint(x, pltpu.HBM)


def body(n_slab, n, panels, block_phase, target_owner, target_cell, target_offset):
    n_dev = n_slab * n
    channels = panels.shape[0]
    nblk = block_phase.shape[1]
    order = panels.shape[1] // nblk
    cols = order * nblk
    targets = target_cell.shape[0]
    (mh, ml), gain, taps = tables(order, nblk)
    vmem = pl.BlockSpec(memory_space=pltpu.VMEM)
    hbm = pl.BlockSpec(memory_space=pl.ANY)
    deep = n * cols
    ready = pl.pallas_call(
        functools.partial(prepare_kernel, n, n_dev, order, nblk),
        out_shape=(
            pltpu.VMEM((n, channels, cols), F32),
            pltpu.VMEM((n, 2, cols), jnp.int32),
            pltpu.VMEM((deep, 2 * TILE), BF16),
            pltpu.VMEM((deep, 2 * TILE), F8),
            pltpu.VMEM((deep, 2 * TILE), F8),
            pltpu.VMEM((order, TAPS, targets), BF16),
            pltpu.VMEM((order, 2 * TAPS, targets), F8),
            pltpu.VMEM((n * 2 * nblk, TAPS), BF16),
            pltpu.VMEM((n * 2 * nblk, 2 * TAPS), F8),
            pltpu.VMEM((n * nblk, targets), F32),
            pltpu.VMEM((n * nblk, targets), F32),
            pltpu.VMEM((2, TILES, cols, cols), BF16),
        ),
        in_specs=[hbm] * 8,
        out_specs=(vmem,) * 12,
        scratch_shapes=[
            pltpu.VMEM((n, 2, nblk), jnp.int32),
            pltpu.VMEM((1, targets), jnp.int32),
            pltpu.VMEM((1, targets), jnp.int32),
            pltpu.VMEM((1, targets), jnp.int32),
            pltpu.VMEM((2 * TAPS, OFFQ), BF16),
            pltpu.SemaphoreType.DMA((6,)),
            pltpu.SemaphoreType.DMA((2,)),
            pltpu.SemaphoreType.DMA((2, n)),
            pltpu.SemaphoreType.DMA((2, n)),
            pltpu.SemaphoreType.DMA((n,)),
            pltpu.SemaphoreType.DMA((n,)),
            pltpu.VMEM((n, nblk, 256), jnp.int32),
            pltpu.VMEM((TAPS, targets), F32),
        ],
        compiler_params=pltpu.CompilerParams(
            collective_id=0, has_side_effects=True, vmem_limit_bytes=8 << 20
        ),
    )(
        *map(
            in_hbm,
            (
                panels,
                block_phase,
                target_owner.reshape(1, targets),
                target_cell.reshape(1, targets),
                target_offset.reshape(1, targets),
                jnp.asarray(taps),
                jnp.asarray(mh),
                jnp.asarray(ml),
            ),
        )
    )
    return pl.pallas_call(
        functools.partial(product_kernel, n, order, nblk, gain),
        out_shape=(
            jax.ShapeDtypeStruct((channels, GS), F32),
            jax.ShapeDtypeStruct((channels, targets), F32),
        ),
        in_specs=[vmem] * 12,
        out_specs=(hbm, vmem),
        scratch_shapes=[
            pltpu.SemaphoreType.DMA((GS // LANES,)),
            pltpu.VMEM((channels, GS), F32),
            pltpu.VMEM((n, 2, 8, cols), F32),
            pltpu.VMEM((2 * n * channels, cols), BF16),
            pltpu.VMEM((TILES * channels, deep), BF16),
            pltpu.VMEM((TILES * channels, deep), F8),
            pltpu.VMEM((TILES * channels, deep), F8),
            pltpu.VMEM((channels, deep), BF16),
            pltpu.VMEM((channels, deep), F8),
            pltpu.VMEM((channels, deep), F8),
            pltpu.VMEM((deep, 2 * targets), BF16),
            pltpu.VMEM((deep, 2 * targets), F8),
            pltpu.VMEM((deep, 2 * targets), F8),
        ],
        compiler_params=pltpu.CompilerParams(vmem_limit_bytes=24 << 20),
    )(*ready)


def solution(mesh):
    placed = (
        P(None, "term"),
        P(None, "term"),
        P(("slab", "term"), None),
        P(("slab", "term")),
        P(("slab", "term")),
    )
    return jax.shard_map(
        functools.partial(body, mesh.shape["slab"], mesh.shape["term"]),
        mesh=mesh,
        in_specs=placed,
        out_specs=(P(None, ("slab", "term")), P(None, ("slab", "term"))),
        check_vma=False,
    )
```

```python
import functools
import math

import jax
import jax.numpy as jnp
import ml_dtypes
import numpy as np
from jax import lax
from jax.experimental import pallas as pl
from jax.experimental.pallas import tpu as pltpu
from jax.sharding import PartitionSpec as P

TAPS = 256
OFFQ = 256
GS = 6144
PHASEQ = 4194304
TILE = 1024
TILES = GS // TILE
LANES = 256
MESH = pl.DeviceIdType.MESH
F32 = jnp.float32
BF16 = jnp.bfloat16
F8 = jnp.float8_e4m3fn
WAVE = 256.0
TAP = 256.0
SHIFTED = 64.0
PANEL = 256.0
FINE = 256.0
FIRST = 512


def local_expansion(centers, half, order):
    nodes = np.cos((np.arange(order) + 0.5) * np.pi / order)
    back = np.cos(np.outer(np.arange(order), np.arccos(nodes))) * 2.0 / order
    back[0] *= 0.5
    x = np.asarray(centers, np.float64)[:, None] + half * nodes[None, :]
    tj = np.polynomial.chebyshev.chebvander(x, order - 1)
    return np.einsum("tnj,kn->tjk", tj, back)


def split_np(x):
    hi = x.astype(np.float32).astype(ml_dtypes.bfloat16)
    lo = (x - hi.astype(np.float64)).astype(np.float32).astype(ml_dtypes.bfloat16)
    return hi, lo


def tables(order, nblk):
    half = TILE / GS
    centers = (2.0 * TILE * np.arange(TILES) + TILE) / GS - 1.0
    m = local_expansion(centers, half, order)
    gain = 400.0 / (math.sqrt(2.0) * np.abs(m).sum(1).max())
    eye = np.eye(nblk)
    big = np.einsum("tjk,bc->tbjkc", m * gain, eye).reshape(TILES, order * nblk, order * nblk)
    frac = (np.arange(OFFQ) + 0.5) / OFFQ
    place = np.arange(TAPS)
    dist = (place - TAPS // 2 + 1.0)[:, None] - frac[None, :]
    sign = np.where(place % 2 == 0, 1.0, -1.0)[:, None]
    taps = sign * np.sin(np.pi * frac)[None, :] / (np.pi * dist) * np.exp(-18.0 * dist * dist / (TAPS * TAPS))
    return split_np(big), gain, np.concatenate(split_np(taps * TAP), 0)


def split(x):
    hi = x.astype(BF16)
    return hi, x - hi.astype(F32)


def dot(a, b):
    return jnp.dot(a, b, preferred_element_type=F32)


def sincos(turns):
    turns = turns & (PHASEQ - 1)
    quad = (turns + PHASEQ // 8) >> 20
    r = (turns - (quad << 20)).astype(F32) * (2.0 * math.pi / PHASEQ)
    r2 = r * r
    s = r + r * r2 * (-1 / 6 + r2 * (1 / 120 + r2 * (-1 / 5040 + r2 * (1 / 362880))))
    c = 1.0 + r2 * (-0.5 + r2 * (1 / 24 + r2 * (-1 / 720 + r2 * (1 / 40320))))
    odd = (quad & 1) == 1
    sn = jnp.where(odd, c, s)
    cs = jnp.where(odd, s, c)
    sn = jnp.where((quad & 2) == 2, -sn, sn)
    cs = jnp.where(((quad + 1) & 2) == 2, -cs, cs)
    return sn, cs


def spread_phases(order, nblk, chunks, ph_ref, col_ref, row_ref):
    cols = order * nblk
    many = 2 * len(chunks)
    r = lax.broadcasted_iota(jnp.int32, (3 * nblk, cols), 0)
    c = lax.broadcasted_iota(jnp.int32, (3 * nblk, cols), 1)
    size = jnp.where(r < nblk, 1.0, jnp.where(r < 2 * nblk, 256.0, 65536.0))
    pick = jnp.where(c % nblk == r % nblk, size, 0.0).astype(BF16)
    r = lax.broadcasted_iota(jnp.int32, (nblk, 3 * nblk), 0)
    c = lax.broadcasted_iota(jnp.int32, (nblk, 3 * nblk), 1)
    size = jnp.where(c < nblk, 1.0, jnp.where(c < 2 * nblk, 256.0, 65536.0))
    eye = jnp.where(c % nblk == r, size, 0.0).astype(BF16)
    v = jnp.concatenate([ph_ref[i] for i in chunks] + [jnp.zeros((-many % 16, nblk), jnp.int32)], 0)
    parts = jnp.concatenate([(v & 255).astype(F32), ((v >> 8) & 255).astype(F32), (v >> 16).astype(F32)], 1)
    parts = parts.astype(BF16)
    row = dot(parts, pick).astype(jnp.int32)
    col = lax.dot_general(eye, parts, (((1,), (1,)), ((), ())), preferred_element_type=F32).astype(jnp.int32)
    for a, i in enumerate(chunks):
        row_ref[i] = row[2 * a : 2 * a + 2]
        col_ref[i, :, 0:128] = jnp.broadcast_to(col[:, 2 * a : 2 * a + 1], (nblk, 128))
        col_ref[i, :, 128:256] = jnp.broadcast_to(col[:, 2 * a + 1 : 2 * a + 2], (nblk, 128))


def wide(x, width):
    return jnp.concatenate([x] * (width // 128), 1)


def taper_targets(n_dev, order, own_ref, cell_ref, off_ref, tap_ref, kern_ref, th, t8):
    count = own_ref.shape[1]
    hot = (lax.broadcasted_iota(jnp.int32, (OFFQ, count), 0) == off_ref[...]).astype(F32).astype(BF16)
    kern = dot(tap_ref[...], hot)
    kern_ref[...] = kern[:TAPS] + kern[TAPS:]

    def rows(r, carry):
        at = pl.multiple_of(r * 32, 32)
        low = pl.multiple_of(TAPS + r * 32, 32)
        for l0 in range(0, count, LANES):
            ll = slice(l0, l0 + LANES)
            owner = own_ref[:, ll]
            first = jnp.where(owner == 0, 0, -GS)
            last = jnp.where(owner == n_dev - 1, GS, 2 * GS)
            pos = lax.broadcasted_iota(jnp.int32, (32, LANES), 0) + (cell_ref[:, ll] + (at - (TAPS // 2 - 1)))
            valid = (pos >= first) & (pos < last)
            m = jnp.where(pos < 0, pos + GS, pos)
            m = jnp.where(m >= GS, m - GS, m)
            x = (2 * m + 1).astype(F32) * (1.0 / GS) - 1.0
            before = jnp.where(valid, kern_ref[pl.ds(at, 32), ll], 0.0)
            now = x * before
            x2 = x + x
            for j in range(order):
                hi, lo = split(before)
                th[j, pl.ds(at, 32), ll] = hi
                t8[j, pl.ds(at, 32), ll] = hi.astype(F8)
                t8[j, pl.ds(low, 32), ll] = lo.astype(F8)
                before, now = now, x2 * now - before
        return carry

    return rows


def fill_basis(order, nblk, i, start, col_ref, bh, b8h, b8l):
    width = bh.shape[1] // 2
    for l0 in range(0, width, LANES):
        lane = lax.broadcasted_iota(jnp.int32, (nblk, LANES), 1) + (start + l0)
        sn, cs = sincos(lane * wide(col_ref[i, :, 128:256], LANES))
        y = (2 * lane + 1).astype(F32) * (1.0 / TILE) - 1.0
        y2 = y + y
        waves = (cs * WAVE, sn * WAVE)
        before, now = jnp.ones_like(y), y
        for k in range(0, order, 2):
            at = pl.multiple_of(i * order * nblk + k * nblk, 32)
            for part, wave in enumerate(waves):
                ll = slice(part * width + l0, part * width + l0 + LANES)
                hi, lo = split(jnp.concatenate([wave * before, wave * now], 0))
                bh[pl.ds(at, 2 * nblk), ll] = hi
                b8h[pl.ds(at, 2 * nblk), ll] = hi.astype(F8)
                b8l[pl.ds(at, 2 * nblk), ll] = lo.astype(F8)
            before = y2 * now - before
            now = y2 * before - now


def fill_waves(nblk, i, col_ref, eh, e8):
    lane = lax.broadcasted_iota(jnp.int32, (nblk, TAPS), 1)
    sn, cs = sincos(lane * wide(col_ref[i, :, 128:256], TAPS))
    at = pl.multiple_of(i * 2 * nblk, 2 * nblk)
    hi, lo = split(jnp.concatenate([cs, sn], 0) * WAVE)
    eh[pl.ds(at, 2 * nblk), :] = hi
    e8[pl.ds(at, 2 * nblk), 0:TAPS] = lo.astype(F8)
    e8[pl.ds(at, 2 * nblk), TAPS : 2 * TAPS] = hi.astype(F8)


def first_phases(nblk, i, first, col_ref, c1, s1):
    count = first.shape[1]
    sn, cs = sincos(wide(col_ref[i, :, 0:128], count) + first * wide(col_ref[i, :, 128:256], count))
    at = pl.multiple_of(i * nblk, nblk)
    c1[pl.ds(at, nblk), :] = cs * (SHIFTED / (WAVE * TAP))
    s1[pl.ds(at, nblk), :] = sn * (SHIFTED / (WAVE * TAP))


def prepare_kernel(
    n, n_dev, order, nblk,
    pan_hbm, ph_hbm, own_hbm, cell_hbm, off_hbm, tap_hbm, mh_hbm, ml_hbm,
    pan_ref, row_ref, col_ref, bh, b8h, b8l, th, t8, eh, e8, c1, s1, m_ref,
    ph_ref, own_ref, cell_ref, off_ref, tap_ref,
    load_sem, own_sem, send_sem, recv_sem, pass_sem, got_sem,
    kern_ref,
):
    cols = order * nblk
    rows = pan_ref.shape[1]
    half = rows // 2
    count = own_ref.shape[1]
    me = lax.axis_index("term")
    slab = lax.axis_index("slab")
    core = lax.rem(slab, 2)
    twin = {"slab": slab + 1 - 2 * core}
    mine = pl.ds(pl.multiple_of(core * half, half), half)
    barrier = pltpu.get_barrier_semaphore()
    for d in range(1, n):
        pl.semaphore_signal(barrier, inc=1, device_id={"term": lax.rem(me + d, n)}, device_id_type=MESH)
    pl.semaphore_signal(barrier, inc=1, device_id=twin, device_id_type=MESH)
    loads = [
        pltpu.make_async_copy(src, dst, load_sem.at[a])
        for a, (src, dst) in enumerate(
            (
                (own_hbm, own_ref), (cell_hbm, cell_ref), (off_hbm, off_ref), (tap_hbm, tap_ref),
                (mh_hbm, m_ref.at[0]), (ml_hbm, m_ref.at[1]),
            )
        )
    ]
    for copy in loads[:4]:
        copy.start()
    owned = [
        pltpu.make_async_copy(src, dst.at[me], own_sem.at[a])
        for a, (src, dst) in enumerate(((pan_hbm, pan_ref), (ph_hbm, ph_ref)))
    ]
    for copy in owned:
        copy.start()
    for copy in loads[:4]:
        copy.wait()
    taper = taper_targets(n_dev, order, own_ref, cell_ref, off_ref, tap_ref, kern_ref, th, t8)
    pl.semaphore_wait(barrier, n)
    bigs, smalls = [], []
    for d in sorted(range(1, n), key=lambda d: -min(d, n - d)):
        peer = {"term": lax.rem(me + d, n)}
        smalls.append(
            pltpu.make_async_remote_copy(
                src_ref=ph_hbm, dst_ref=ph_ref.at[me], send_sem=send_sem.at[1, d], recv_sem=recv_sem.at[1, d],
                device_id=peer, device_id_type=MESH,
            )
        )
        bigs.append((
            d,
            pltpu.make_async_remote_copy(
                src_ref=pan_hbm.at[mine], dst_ref=pan_ref.at[me, mine], send_sem=send_sem.at[0, d],
                recv_sem=recv_sem.at[0, d], device_id=peer, device_id_type=MESH,
            ),
        ))
    for small in smalls:
        small.start()
    for _, big in bigs:
        big.start()
    for copy in loads[4:]:
        copy.start()
    lax.fori_loop(0, TAPS // 32, taper, 0)
    first = own_ref[...] * GS + cell_ref[...] - (TAPS // 2 - 1)

    def chunk(d, carry):
        i = lax.rem(me + d, n)
        fill_waves(nblk, i, col_ref, eh, e8)
        first_phases(nblk, i, first, col_ref, c1, s1)
        fill_basis(order, nblk, i, 0, col_ref, bh, b8h, b8l)
        return carry

    owned[1].wait()
    spread_phases(order, nblk, [me], ph_ref, col_ref, row_ref)
    lax.fori_loop(0, 1, chunk, 0)
    for small in smalls:
        small.wait_recv()
    spread_phases(order, nblk, [lax.rem(me + d, n) for d in range(1, n)], ph_ref, col_ref, row_ref)
    lax.fori_loop(1, n - 1, chunk, 0)
    passes = []
    for d, big in reversed(bigs):
        big.wait_recv()
        origin = lax.rem(me - d + n, n)
        passed = pltpu.make_async_remote_copy(
            src_ref=pan_ref.at[origin, mine], dst_ref=pan_ref.at[origin, mine],
            send_sem=pass_sem.at[d], recv_sem=got_sem.at[d], device_id=twin, device_id_type=MESH,
        )
        passed.start()
        passes.append(passed)
    lax.fori_loop(n - 1, n, chunk, 0)
    for copy in loads[4:]:
        copy.wait()
    owned[0].wait()
    for passed in passes:
        passed.wait()
    for small in smalls:
        small.wait_send()
    for _, big in bigs:
        big.wait_send()


def moments(n, nblk, order, j2, th, t8, eh, e8, c1, s1, vh, v8h, v8l):
    cols = order * nblk
    count = c1.shape[1]
    for l0 in range(0, count, LANES):
        ll = slice(l0, l0 + LANES)
        v = [dot(eh[...], th[2 * j2 + a, :, ll]) + dot(e8[...], t8[2 * j2 + a, :, ll]) for a in range(2)]
        for i in range(n):
            at = slice(i * cols + j2 * 2 * nblk, i * cols + (j2 + 1) * 2 * nblk)
            cs = c1[i * nblk : (i + 1) * nblk, ll]
            sn = s1[i * nblk : (i + 1) * nblk, ll]
            vc = [u[i * 2 * nblk : i * 2 * nblk + nblk] for u in v]
            vs = [u[i * 2 * nblk + nblk : (i + 1) * 2 * nblk] for u in v]
            re = jnp.concatenate([cs * a - sn * b for a, b in zip(vc, vs)], 0)
            im = jnp.concatenate([sn * a + cs * b for a, b in zip(vc, vs)], 0)
            for part, w in enumerate((re, im)):
                lp = slice(part * count + l0, part * count + l0 + LANES)
                hi, lo = split(w)
                vh[at, lp] = hi
                v8h[at, lp] = hi.astype(F8)
                v8l[at, lp] = lo.astype(F8)


def scales(top):
    top = jnp.full((8, 128), jnp.maximum(top, 1e-30), F32)
    return 1.0 / top, top


def spread_rows(x, rows):
    return jnp.concatenate([x] * (rows // 8), 0)


def both_halves(x):
    hi, lo = split(x)
    return hi, lo.astype(BF16)


def spun(d, spin, row_ref, spin_ref):
    sn, cs = sincos(row_ref[d, 0:1, :] + spin * row_ref[d, 1:2, :])
    spin_ref[d, 0] = sn
    spin_ref[d, 1] = cs


def rotate_tile(rows, slots, t, both_ref, scale, spin_ref, m_ref, ah, a8h, a8l):
    half = rows // 2
    cols = both_ref.shape[1]
    many = len(slots) * rows
    z2 = dot(both_ref[...], m_ref[0, t])
    z2 = z2[:many] + z2[many:] + dot(both_ref[0:many, :], m_ref[1, t])
    rr = slice(t * rows, (t + 1) * rows)
    for a, d in enumerate(slots):
        z = z2[a * rows : (a + 1) * rows]
        zr, zi = z[:half], z[half:]
        by = wide(scale[0:1], cols)
        st = spin_ref[d, 0, t : t + 1, :] * by
        ct = spin_ref[d, 1, t : t + 1, :] * by
        hi, lo = split(jnp.concatenate([ct * zr - st * zi, ct * zi + st * zr], 0))
        at = slice(a * cols, (a + 1) * cols)
        ah[rr, at] = hi
        a8h[rr, at] = hi.astype(F8)
        a8l[rr, at] = (lo * FINE).astype(F8)


def product_kernel(
    n, order, nblk, gain,
    pan_ref, row_ref, col_ref, bh, b8h, b8l, th, t8, eh, e8, c1, s1, m_ref,
    grid_out, val_out,
    store_sem, grid_ref, val_ref, spin_ref, both_ref, ah, a8h, a8l, ph, p8h, p8l, vh, v8h, v8l, ch, c8h, c8l,
):
    cols = order * nblk
    rows = pan_ref.shape[1]
    half = rows // 2
    count = val_ref.shape[1]
    r = lax.broadcasted_iota(jnp.int32, (cols, cols), 0)
    c = lax.broadcasted_iota(jnp.int32, (cols, cols), 1)
    perm = ((r % order == c // nblk) & (r // order == c % nblk)).astype(F32).astype(BF16)
    base = (lax.axis_index("slab") * n + lax.axis_index("term")) * GS
    top = jnp.max(jnp.abs(pan_ref[0]))
    for i in range(1, n):
        top = jnp.maximum(top, jnp.max(jnp.abs(pan_ref[i])))
    scale, unscale = scales(top)
    spin = lax.broadcasted_iota(jnp.int32, (8, cols), 0) * TILE + base
    for i in range(n):
        spun(i, spin, row_ref, spin_ref)
        hi, lo = both_halves(pan_ref[i])
        both_ref[i * rows : (i + 1) * rows] = hi
        both_ref[(n + i) * rows : (n + i + 1) * rows] = lo
    for t in range(TILES):
        rotate_tile(rows, list(range(n)), t, both_ref, scale, spin_ref, m_ref, ah, a8h, a8l)
    pp = dot(both_ref[...], perm)
    pp = pp[: n * rows] + pp[n * rows :]
    for i in range(n):
        hi, lo = split(pp[i * rows : (i + 1) * rows] * (spread_rows(wide(scale, cols), rows) * PANEL))
        at = slice(i * cols, (i + 1) * cols)
        ph[:, at] = hi
        p8h[:, at] = hi.astype(F8)
        p8l[:, at] = (lo * FINE).astype(F8)

    down = wide(unscale, LANES) * (1.0 / (WAVE * gain))
    down = jnp.concatenate([down] * (half // 8), 0)
    pairs = order // 2
    chunks = TILE // LANES
    early = chunks - 1
    whole = FIRST // LANES
    stores = []
    for chunk in range(chunks):
        if chunk == early:
            back = spread_rows(wide(unscale, count) * (1.0 / (SHIFTED * PANEL)), half)
            x = dot(ph[...], vh[...]) + dot(p8h[...], v8l[...]) + dot(p8l[...], v8h[...]) * (1.0 / FINE)
            val_ref[:half] = (x[:half, :count] - x[half:, count:]) * back
            val_ref[half:] = (x[half:, :count] + x[:half, count:]) * back
            store = pltpu.make_async_copy(val_ref, val_out, store_sem.at[chunks * TILES])
            store.start()
            stores.append(store)
        acc = []
        for part in range(2):
            lo_col, width, (h, h8, l8) = chunk * LANES, FIRST, (bh, b8h, b8l)
            if lo_col >= FIRST:
                lo_col, width, (h, h8, l8) = lo_col - FIRST, TILE - FIRST, (ch, c8h, c8l)
            cc = slice(part * width + lo_col, part * width + lo_col + LANES)
            x = dot(ah[...], h[:, cc]) + dot(a8h[...], l8[:, cc])
            acc.append(x + dot(a8l[...], h8[:, cc]) * (1.0 / FINE))
        for i in range(chunk * n // whole, (chunk + 1) * n // whole if chunk < whole else 0):
            fill_basis(order, nblk, i, FIRST, col_ref, ch, c8h, c8l)
        for j2 in range(-(-chunk * pairs // early), min(pairs, -(-(chunk + 1) * pairs // early))):
            moments(n, nblk, order, j2, th, t8, eh, e8, c1, s1, vh, v8h, v8l)
        for t in range(TILES):
            cc = slice(t * TILE + chunk * LANES, t * TILE + (chunk + 1) * LANES)
            a, b = t * rows, t * rows + half
            grid_ref[:half, cc] = (acc[0][a:b] - acc[1][b : b + half]) * down
            grid_ref[half:, cc] = (acc[0][b : b + half] + acc[1][a:b]) * down
            store = pltpu.make_async_copy(grid_ref.at[:, cc], grid_out.at[:, cc], store_sem.at[chunk * TILES + t])
            store.start()
            stores.append(store)
    for store in stores:
        store.wait()


def in_hbm(x):
    return pltpu.with_memory_space_constraint(x, pltpu.HBM)


def body(n_slab, n, panels, block_phase, target_owner, target_cell, target_offset):
    n_dev = n_slab * n
    channels = panels.shape[0]
    nblk = block_phase.shape[1]
    order = panels.shape[1] // nblk
    cols = order * nblk
    targets = target_cell.shape[0]
    (mh, ml), gain, taps = tables(order, nblk)
    vmem = pl.BlockSpec(memory_space=pltpu.VMEM)
    hbm = pl.BlockSpec(memory_space=pl.ANY)
    deep = n * cols
    ready = pl.pallas_call(
        functools.partial(prepare_kernel, n, n_dev, order, nblk),
        out_shape=(
            pltpu.VMEM((n, channels, cols), F32),
            pltpu.VMEM((n, 2, cols), jnp.int32),
            pltpu.VMEM((n, nblk, 256), jnp.int32),
            pltpu.VMEM((deep, 2 * FIRST), BF16),
            pltpu.VMEM((deep, 2 * FIRST), F8),
            pltpu.VMEM((deep, 2 * FIRST), F8),
            pltpu.VMEM((order, TAPS, targets), BF16),
            pltpu.VMEM((order, 2 * TAPS, targets), F8),
            pltpu.VMEM((n * 2 * nblk, TAPS), BF16),
            pltpu.VMEM((n * 2 * nblk, 2 * TAPS), F8),
            pltpu.VMEM((n * nblk, targets), F32),
            pltpu.VMEM((n * nblk, targets), F32),
            pltpu.VMEM((2, TILES, cols, cols), BF16),
        ),
        in_specs=[hbm] * 8,
        out_specs=(vmem,) * 13,
        scratch_shapes=[
            pltpu.VMEM((n, 2, nblk), jnp.int32),
            pltpu.VMEM((1, targets), jnp.int32),
            pltpu.VMEM((1, targets), jnp.int32),
            pltpu.VMEM((1, targets), jnp.int32),
            pltpu.VMEM((2 * TAPS, OFFQ), BF16),
            pltpu.SemaphoreType.DMA((6,)),
            pltpu.SemaphoreType.DMA((2,)),
            pltpu.SemaphoreType.DMA((2, n)),
            pltpu.SemaphoreType.DMA((2, n)),
            pltpu.SemaphoreType.DMA((n,)),
            pltpu.SemaphoreType.DMA((n,)),
            pltpu.VMEM((TAPS, targets), F32),
        ],
        compiler_params=pltpu.CompilerParams(
            collective_id=0, has_side_effects=True, vmem_limit_bytes=8 << 20
        ),
    )(
        *map(
            in_hbm,
            (
                panels,
                block_phase,
                target_owner.reshape(1, targets),
                target_cell.reshape(1, targets),
                target_offset.reshape(1, targets),
                jnp.asarray(taps),
                jnp.asarray(mh),
                jnp.asarray(ml),
            ),
        )
    )
    return pl.pallas_call(
        functools.partial(product_kernel, n, order, nblk, gain),
        out_shape=(
            jax.ShapeDtypeStruct((channels, GS), F32),
            jax.ShapeDtypeStruct((channels, targets), F32),
        ),
        in_specs=[vmem] * 13,
        out_specs=(hbm, hbm),
        scratch_shapes=[
            pltpu.SemaphoreType.DMA((GS // LANES + 1,)),
            pltpu.VMEM((channels, GS), F32),
            pltpu.VMEM((channels, targets), F32),
            pltpu.VMEM((n, 2, 8, cols), F32),
            pltpu.VMEM((2 * n * channels, cols), BF16),
            pltpu.VMEM((TILES * channels, deep), BF16),
            pltpu.VMEM((TILES * channels, deep), F8),
            pltpu.VMEM((TILES * channels, deep), F8),
            pltpu.VMEM((channels, deep), BF16),
            pltpu.VMEM((channels, deep), F8),
            pltpu.VMEM((channels, deep), F8),
            pltpu.VMEM((deep, 2 * targets), BF16),
            pltpu.VMEM((deep, 2 * targets), F8),
            pltpu.VMEM((deep, 2 * targets), F8),
            pltpu.VMEM((deep, 2 * (TILE - FIRST)), BF16),
            pltpu.VMEM((deep, 2 * (TILE - FIRST)), F8),
            pltpu.VMEM((deep, 2 * (TILE - FIRST)), F8),
        ],
        compiler_params=pltpu.CompilerParams(vmem_limit_bytes=24 << 20),
    )(*ready)


def solution(mesh):
    placed = (
        P(None, "term"),
        P(None, "term"),
        P(("slab", "term"), None),
        P(("slab", "term")),
        P(("slab", "term")),
    )
    return jax.shard_map(
        functools.partial(body, mesh.shape["slab"], mesh.shape["term"]),
        mesh=mesh,
        in_specs=placed,
        out_specs=(P(None, ("slab", "term")), P(None, ("slab", "term"))),
        check_vma=False,
    )
```

```python
import functools
import math

import jax
import jax.numpy as jnp
import ml_dtypes
import numpy as np
from jax import lax
from jax.experimental import pallas as pl
from jax.experimental.pallas import tpu as pltpu
from jax.sharding import PartitionSpec as P

TAPS = 256
OFFQ = 256
GS = 6144
PHASEQ = 4194304
TILE = 1024
TILES = GS // TILE
LANES = 256
MESH = pl.DeviceIdType.MESH
F32 = jnp.float32
BF16 = jnp.bfloat16
F8 = jnp.float8_e4m3fn
WAVE = 256.0
TAP = 256.0
SHIFTED = 64.0
PANEL = 256.0
FINE = 256.0
FIRST = 256


def local_expansion(centers, half, order):
    nodes = np.cos((np.arange(order) + 0.5) * np.pi / order)
    back = np.cos(np.outer(np.arange(order), np.arccos(nodes))) * 2.0 / order
    back[0] *= 0.5
    x = np.asarray(centers, np.float64)[:, None] + half * nodes[None, :]
    tj = np.polynomial.chebyshev.chebvander(x, order - 1)
    return np.einsum("tnj,kn->tjk", tj, back)


def split_np(x):
    hi = x.astype(np.float32).astype(ml_dtypes.bfloat16)
    lo = (x - hi.astype(np.float64)).astype(np.float32).astype(ml_dtypes.bfloat16)
    return hi, lo


def tables(order, nblk):
    half = TILE / GS
    centers = (2.0 * TILE * np.arange(TILES) + TILE) / GS - 1.0
    m = local_expansion(centers, half, order)
    gain = 400.0 / (math.sqrt(2.0) * np.abs(m).sum(1).max())
    eye = np.eye(nblk)
    big = np.einsum("tjk,bc->tbjkc", m * gain, eye).reshape(TILES, order * nblk, order * nblk)
    frac = (np.arange(OFFQ) + 0.5) / OFFQ
    place = np.arange(TAPS)
    dist = (place - TAPS // 2 + 1.0)[:, None] - frac[None, :]
    sign = np.where(place % 2 == 0, 1.0, -1.0)[:, None]
    taps = sign * np.sin(np.pi * frac)[None, :] / (np.pi * dist) * np.exp(-18.0 * dist * dist / (TAPS * TAPS))
    return split_np(big), gain, np.concatenate(split_np(taps * TAP), 0)


def split(x):
    hi = x.astype(BF16)
    return hi, x - hi.astype(F32)


def dot(a, b):
    return jnp.dot(a, b, preferred_element_type=F32)


def sincos(turns):
    turns = turns & (PHASEQ - 1)
    quad = (turns + PHASEQ // 8) >> 20
    r = (turns - (quad << 20)).astype(F32) * (2.0 * math.pi / PHASEQ)
    r2 = r * r
    s = r + r * r2 * (-1 / 6 + r2 * (1 / 120 + r2 * (-1 / 5040 + r2 * (1 / 362880))))
    c = 1.0 + r2 * (-0.5 + r2 * (1 / 24 + r2 * (-1 / 720 + r2 * (1 / 40320))))
    odd = (quad & 1) == 1
    sn = jnp.where(odd, c, s)
    cs = jnp.where(odd, s, c)
    sn = jnp.where((quad & 2) == 2, -sn, sn)
    cs = jnp.where(((quad + 1) & 2) == 2, -cs, cs)
    return sn, cs


def spread_phases(order, nblk, chunks, ph_ref, col_ref, row_ref):
    cols = order * nblk
    many = 2 * len(chunks)
    r = lax.broadcasted_iota(jnp.int32, (3 * nblk, cols), 0)
    c = lax.broadcasted_iota(jnp.int32, (3 * nblk, cols), 1)
    size = jnp.where(r < nblk, 1.0, jnp.where(r < 2 * nblk, 256.0, 65536.0))
    pick = jnp.where(c % nblk == r % nblk, size, 0.0).astype(BF16)
    r = lax.broadcasted_iota(jnp.int32, (nblk, 3 * nblk), 0)
    c = lax.broadcasted_iota(jnp.int32, (nblk, 3 * nblk), 1)
    size = jnp.where(c < nblk, 1.0, jnp.where(c < 2 * nblk, 256.0, 65536.0))
    eye = jnp.where(c % nblk == r, size, 0.0).astype(BF16)
    v = jnp.concatenate([ph_ref[i] for i in chunks] + [jnp.zeros((-many % 16, nblk), jnp.int32)], 0)
    parts = jnp.concatenate([(v & 255).astype(F32), ((v >> 8) & 255).astype(F32), (v >> 16).astype(F32)], 1)
    parts = parts.astype(BF16)
    row = dot(parts, pick).astype(jnp.int32)
    col = lax.dot_general(eye, parts, (((1,), (1,)), ((), ())), preferred_element_type=F32).astype(jnp.int32)
    for a, i in enumerate(chunks):
        row_ref[i] = row[2 * a : 2 * a + 2]
        col_ref[i, :, 0:128] = jnp.broadcast_to(col[:, 2 * a : 2 * a + 1], (nblk, 128))
        col_ref[i, :, 128:256] = jnp.broadcast_to(col[:, 2 * a + 1 : 2 * a + 2], (nblk, 128))


def wide(x, width):
    return jnp.concatenate([x] * (width // 128), 1)


def taper_targets(n_dev, order, own_ref, cell_ref, off_ref, tap_ref, kern_ref, th, t8):
    count = own_ref.shape[1]
    hot = (lax.broadcasted_iota(jnp.int32, (OFFQ, count), 0) == off_ref[...]).astype(F32).astype(BF16)
    kern = dot(tap_ref[...], hot)
    kern_ref[...] = kern[:TAPS] + kern[TAPS:]

    def rows(r, carry):
        at = pl.multiple_of(r * 32, 32)
        low = pl.multiple_of(TAPS + r * 32, 32)
        for l0 in range(0, count, LANES):
            ll = slice(l0, l0 + LANES)
            owner = own_ref[:, ll]
            first = jnp.where(owner == 0, 0, -GS)
            last = jnp.where(owner == n_dev - 1, GS, 2 * GS)
            pos = lax.broadcasted_iota(jnp.int32, (32, LANES), 0) + (cell_ref[:, ll] + (at - (TAPS // 2 - 1)))
            valid = (pos >= first) & (pos < last)
            m = jnp.where(pos < 0, pos + GS, pos)
            m = jnp.where(m >= GS, m - GS, m)
            x = (2 * m + 1).astype(F32) * (1.0 / GS) - 1.0
            before = jnp.where(valid, kern_ref[pl.ds(at, 32), ll], 0.0)
            now = x * before
            x2 = x + x
            for j in range(order):
                hi, lo = split(before)
                th[j, pl.ds(at, 32), ll] = hi
                t8[j, pl.ds(at, 32), ll] = hi.astype(F8)
                t8[j, pl.ds(low, 32), ll] = lo.astype(F8)
                before, now = now, x2 * now - before
        return carry

    return rows


def fill_basis(order, nblk, i, start, col_ref, bh, b8h, b8l):
    width = bh.shape[1] // 2
    for l0 in range(0, width, LANES):
        lane = lax.broadcasted_iota(jnp.int32, (nblk, LANES), 1) + (start + l0)
        sn, cs = sincos(lane * wide(col_ref[i, :, 128:256], LANES))
        y = (2 * lane + 1).astype(F32) * (1.0 / TILE) - 1.0
        y2 = y + y
        waves = (cs * WAVE, sn * WAVE)
        before, now = jnp.ones_like(y), y
        for k in range(0, order, 2):
            at = pl.multiple_of(i * order * nblk + k * nblk, 32)
            for part, wave in enumerate(waves):
                ll = slice(part * width + l0, part * width + l0 + LANES)
                hi, lo = split(jnp.concatenate([wave * before, wave * now], 0))
                bh[pl.ds(at, 2 * nblk), ll] = hi
                b8h[pl.ds(at, 2 * nblk), ll] = hi.astype(F8)
                b8l[pl.ds(at, 2 * nblk), ll] = lo.astype(F8)
            before = y2 * now - before
            now = y2 * before - now


def fill_waves(nblk, i, col_ref, eh, e8):
    lane = lax.broadcasted_iota(jnp.int32, (nblk, TAPS), 1)
    sn, cs = sincos(lane * wide(col_ref[i, :, 128:256], TAPS))
    at = pl.multiple_of(i * 2 * nblk, 2 * nblk)
    hi, lo = split(jnp.concatenate([cs, sn], 0) * WAVE)
    eh[pl.ds(at, 2 * nblk), :] = hi
    e8[pl.ds(at, 2 * nblk), 0:TAPS] = lo.astype(F8)
    e8[pl.ds(at, 2 * nblk), TAPS : 2 * TAPS] = hi.astype(F8)


def first_phases(nblk, i, first, col_ref, c1, s1):
    count = first.shape[1]
    sn, cs = sincos(wide(col_ref[i, :, 0:128], count) + first * wide(col_ref[i, :, 128:256], count))
    at = pl.multiple_of(i * nblk, nblk)
    c1[pl.ds(at, nblk), :] = cs * (SHIFTED / (WAVE * TAP))
    s1[pl.ds(at, nblk), :] = sn * (SHIFTED / (WAVE * TAP))


def prepare_kernel(
    n, n_dev, order, nblk,
    pan_hbm, ph_hbm, own_hbm, cell_hbm, off_hbm, tap_hbm, mh_hbm, ml_hbm,
    pan_ref, row_ref, col_ref, bh, b8h, b8l, th, t8, eh, e8, c1, s1, m_ref,
    ph_ref, own_ref, cell_ref, off_ref, tap_ref,
    load_sem, own_sem, send_sem, recv_sem, pass_sem, got_sem,
    kern_ref,
):
    cols = order * nblk
    rows = pan_ref.shape[1]
    half = rows // 2
    count = own_ref.shape[1]
    me = lax.axis_index("term")
    slab = lax.axis_index("slab")
    core = lax.rem(slab, 2)
    twin = {"slab": slab + 1 - 2 * core}
    mine = pl.ds(pl.multiple_of(core * half, half), half)
    barrier = pltpu.get_barrier_semaphore()
    for d in range(1, n):
        pl.semaphore_signal(barrier, inc=1, device_id={"term": lax.rem(me + d, n)}, device_id_type=MESH)
    pl.semaphore_signal(barrier, inc=1, device_id=twin, device_id_type=MESH)
    loads = [
        pltpu.make_async_copy(src, dst, load_sem.at[a])
        for a, (src, dst) in enumerate(
            (
                (own_hbm, own_ref), (cell_hbm, cell_ref), (off_hbm, off_ref), (tap_hbm, tap_ref),
                (mh_hbm, m_ref.at[0]), (ml_hbm, m_ref.at[1]),
            )
        )
    ]
    for copy in loads[:4]:
        copy.start()
    owned = [
        pltpu.make_async_copy(src, dst.at[me], own_sem.at[a])
        for a, (src, dst) in enumerate(((pan_hbm, pan_ref), (ph_hbm, ph_ref)))
    ]
    for copy in owned:
        copy.start()
    for copy in loads[:4]:
        copy.wait()
    taper = taper_targets(n_dev, order, own_ref, cell_ref, off_ref, tap_ref, kern_ref, th, t8)
    pl.semaphore_wait(barrier, n)
    bigs, smalls = [], []
    for d in sorted(range(1, n), key=lambda d: -min(d, n - d)):
        peer = {"term": lax.rem(me + d, n)}
        smalls.append(
            pltpu.make_async_remote_copy(
                src_ref=ph_hbm, dst_ref=ph_ref.at[me], send_sem=send_sem.at[1, d], recv_sem=recv_sem.at[1, d],
                device_id=peer, device_id_type=MESH,
            )
        )
        bigs.append((
            d,
            pltpu.make_async_remote_copy(
                src_ref=pan_hbm.at[mine], dst_ref=pan_ref.at[me, mine], send_sem=send_sem.at[0, d],
                recv_sem=recv_sem.at[0, d], device_id=peer, device_id_type=MESH,
            ),
        ))
    for small in smalls:
        small.start()
    for _, big in bigs:
        big.start()
    for copy in loads[4:]:
        copy.start()
    lax.fori_loop(0, TAPS // 32, taper, 0)
    first = own_ref[...] * GS + cell_ref[...] - (TAPS // 2 - 1)

    def chunk(d, carry):
        i = lax.rem(me + d, n)
        fill_waves(nblk, i, col_ref, eh, e8)
        first_phases(nblk, i, first, col_ref, c1, s1)
        fill_basis(order, nblk, i, 0, col_ref, bh, b8h, b8l)
        return carry

    owned[1].wait()
    spread_phases(order, nblk, [me], ph_ref, col_ref, row_ref)
    lax.fori_loop(0, 1, chunk, 0)
    for small in smalls:
        small.wait_recv()
    spread_phases(order, nblk, [lax.rem(me + d, n) for d in range(1, n)], ph_ref, col_ref, row_ref)
    lax.fori_loop(1, n - 1, chunk, 0)
    passes = []
    for d, big in reversed(bigs):
        big.wait_recv()
        origin = lax.rem(me - d + n, n)
        passed = pltpu.make_async_remote_copy(
            src_ref=pan_ref.at[origin, mine], dst_ref=pan_ref.at[origin, mine],
            send_sem=pass_sem.at[d], recv_sem=got_sem.at[d], device_id=twin, device_id_type=MESH,
        )
        passed.start()
        passes.append(passed)
    lax.fori_loop(n - 1, n, chunk, 0)
    for copy in loads[4:]:
        copy.wait()
    owned[0].wait()
    for passed in passes:
        passed.wait()
    for small in smalls:
        small.wait_send()
    for _, big in bigs:
        big.wait_send()


def moments(n, nblk, order, j2, th, t8, eh, e8, c1, s1, vh, v8h, v8l):
    cols = order * nblk
    count = c1.shape[1]
    for l0 in range(0, count, LANES):
        ll = slice(l0, l0 + LANES)
        v = [dot(eh[...], th[2 * j2 + a, :, ll]) + dot(e8[...], t8[2 * j2 + a, :, ll]) for a in range(2)]
        for i in range(n):
            at = slice(i * cols + j2 * 2 * nblk, i * cols + (j2 + 1) * 2 * nblk)
            cs = c1[i * nblk : (i + 1) * nblk, ll]
            sn = s1[i * nblk : (i + 1) * nblk, ll]
            vc = [u[i * 2 * nblk : i * 2 * nblk + nblk] for u in v]
            vs = [u[i * 2 * nblk + nblk : (i + 1) * 2 * nblk] for u in v]
            re = jnp.concatenate([cs * a - sn * b for a, b in zip(vc, vs)], 0)
            im = jnp.concatenate([sn * a + cs * b for a, b in zip(vc, vs)], 0)
            for part, w in enumerate((re, im)):
                lp = slice(part * count + l0, part * count + l0 + LANES)
                hi, lo = split(w)
                vh[at, lp] = hi
                v8h[at, lp] = hi.astype(F8)
                v8l[at, lp] = lo.astype(F8)


def scales(top):
    top = jnp.full((8, 128), jnp.maximum(top, 1e-30), F32)
    return 1.0 / top, top


def spread_rows(x, rows):
    return jnp.concatenate([x] * (rows // 8), 0)


def both_halves(x):
    hi, lo = split(x)
    return hi, lo.astype(BF16)


def spun(d, spin, row_ref, spin_ref):
    sn, cs = sincos(row_ref[d, 0:1, :] + spin * row_ref[d, 1:2, :])
    spin_ref[d, 0] = sn
    spin_ref[d, 1] = cs


def rotate_tile(rows, slots, t, both_ref, scale, spin_ref, m_ref, ah, a8h, a8l):
    half = rows // 2
    cols = both_ref.shape[1]
    many = len(slots) * rows
    z2 = dot(both_ref[...], m_ref[0, t])
    z2 = z2[:many] + z2[many:] + dot(both_ref[0:many, :], m_ref[1, t])
    rr = slice(t * rows, (t + 1) * rows)
    for a, d in enumerate(slots):
        z = z2[a * rows : (a + 1) * rows]
        zr, zi = z[:half], z[half:]
        by = wide(scale[0:1], cols)
        st = spin_ref[d, 0, t : t + 1, :] * by
        ct = spin_ref[d, 1, t : t + 1, :] * by
        hi, lo = split(jnp.concatenate([ct * zr - st * zi, ct * zi + st * zr], 0))
        at = slice(a * cols, (a + 1) * cols)
        ah[rr, at] = hi
        a8h[rr, at] = hi.astype(F8)
        a8l[rr, at] = (lo * FINE).astype(F8)


def product_kernel(
    n, order, nblk, gain,
    pan_ref, row_ref, col_ref, bh, b8h, b8l, th, t8, eh, e8, c1, s1, m_ref,
    grid_out, val_out,
    store_sem, grid_ref, val_ref, spin_ref, both_ref, ah, a8h, a8l, ph, p8h, p8l, vh, v8h, v8l, ch, c8h, c8l,
):
    cols = order * nblk
    rows = pan_ref.shape[1]
    half = rows // 2
    count = val_ref.shape[1]
    r = lax.broadcasted_iota(jnp.int32, (cols, cols), 0)
    c = lax.broadcasted_iota(jnp.int32, (cols, cols), 1)
    perm = ((r % order == c // nblk) & (r // order == c % nblk)).astype(F32).astype(BF16)
    base = (lax.axis_index("slab") * n + lax.axis_index("term")) * GS
    top = jnp.max(jnp.abs(pan_ref[0]))
    for i in range(1, n):
        top = jnp.maximum(top, jnp.max(jnp.abs(pan_ref[i])))
    scale, unscale = scales(top)
    spin = lax.broadcasted_iota(jnp.int32, (8, cols), 0) * TILE + base
    for i in range(n):
        spun(i, spin, row_ref, spin_ref)
        hi, lo = both_halves(pan_ref[i])
        both_ref[i * rows : (i + 1) * rows] = hi
        both_ref[(n + i) * rows : (n + i + 1) * rows] = lo
    for t in range(TILES):
        rotate_tile(rows, list(range(n)), t, both_ref, scale, spin_ref, m_ref, ah, a8h, a8l)
    pp = dot(both_ref[...], perm)
    pp = pp[: n * rows] + pp[n * rows :]
    for i in range(n):
        hi, lo = split(pp[i * rows : (i + 1) * rows] * (spread_rows(wide(scale, cols), rows) * PANEL))
        at = slice(i * cols, (i + 1) * cols)
        ph[:, at] = hi
        p8h[:, at] = hi.astype(F8)
        p8l[:, at] = (lo * FINE).astype(F8)

    down = wide(unscale, LANES) * (1.0 / (WAVE * gain))
    down = jnp.concatenate([down] * (half // 8), 0)
    pairs = order // 2
    chunks = TILE // LANES
    early = chunks - 1
    whole = FIRST // LANES
    stores = []
    for chunk in range(chunks):
        if chunk == early:
            back = spread_rows(wide(unscale, count) * (1.0 / (SHIFTED * PANEL)), half)
            x = dot(ph[...], vh[...]) + dot(p8h[...], v8l[...]) + dot(p8l[...], v8h[...]) * (1.0 / FINE)
            val_ref[:half] = (x[:half, :count] - x[half:, count:]) * back
            val_ref[half:] = (x[half:, :count] + x[:half, count:]) * back
            store = pltpu.make_async_copy(val_ref, val_out, store_sem.at[chunks * TILES])
            store.start()
            stores.append(store)
        acc = []
        for part in range(2):
            lo_col, width, (h, h8, l8) = chunk * LANES, FIRST, (bh, b8h, b8l)
            if lo_col >= FIRST:
                lo_col, width, (h, h8, l8) = lo_col - FIRST, TILE - FIRST, (ch, c8h, c8l)
            cc = slice(part * width + lo_col, part * width + lo_col + LANES)
            x = dot(ah[...], h[:, cc]) + dot(a8h[...], l8[:, cc])
            acc.append(x + dot(a8l[...], h8[:, cc]) * (1.0 / FINE))
        for i in range(chunk * n // whole, (chunk + 1) * n // whole if chunk < whole else 0):
            fill_basis(order, nblk, i, FIRST, col_ref, ch, c8h, c8l)
        for j2 in range(-(-chunk * pairs // early), min(pairs, -(-(chunk + 1) * pairs // early))):
            moments(n, nblk, order, j2, th, t8, eh, e8, c1, s1, vh, v8h, v8l)
        for t in range(TILES):
            cc = slice(t * TILE + chunk * LANES, t * TILE + (chunk + 1) * LANES)
            a, b = t * rows, t * rows + half
            grid_ref[:half, cc] = (acc[0][a:b] - acc[1][b : b + half]) * down
            grid_ref[half:, cc] = (acc[0][b : b + half] + acc[1][a:b]) * down
            store = pltpu.make_async_copy(grid_ref.at[:, cc], grid_out.at[:, cc], store_sem.at[chunk * TILES + t])
            store.start()
            stores.append(store)
    for store in stores:
        store.wait()


def in_hbm(x):
    return pltpu.with_memory_space_constraint(x, pltpu.HBM)


def body(n_slab, n, panels, block_phase, target_owner, target_cell, target_offset):
    n_dev = n_slab * n
    channels = panels.shape[0]
    nblk = block_phase.shape[1]
    order = panels.shape[1] // nblk
    cols = order * nblk
    targets = target_cell.shape[0]
    (mh, ml), gain, taps = tables(order, nblk)
    vmem = pl.BlockSpec(memory_space=pltpu.VMEM)
    hbm = pl.BlockSpec(memory_space=pl.ANY)
    deep = n * cols
    ready = pl.pallas_call(
        functools.partial(prepare_kernel, n, n_dev, order, nblk),
        out_shape=(
            pltpu.VMEM((n, channels, cols), F32),
            pltpu.VMEM((n, 2, cols), jnp.int32),
            pltpu.VMEM((n, nblk, 256), jnp.int32),
            pltpu.VMEM((deep, 2 * FIRST), BF16),
            pltpu.VMEM((deep, 2 * FIRST), F8),
            pltpu.VMEM((deep, 2 * FIRST), F8),
            pltpu.VMEM((order, TAPS, targets), BF16),
            pltpu.VMEM((order, 2 * TAPS, targets), F8),
            pltpu.VMEM((n * 2 * nblk, TAPS), BF16),
            pltpu.VMEM((n * 2 * nblk, 2 * TAPS), F8),
            pltpu.VMEM((n * nblk, targets), F32),
            pltpu.VMEM((n * nblk, targets), F32),
            pltpu.VMEM((2, TILES, cols, cols), BF16),
        ),
        in_specs=[hbm] * 8,
        out_specs=(vmem,) * 13,
        scratch_shapes=[
            pltpu.VMEM((n, 2, nblk), jnp.int32),
            pltpu.VMEM((1, targets), jnp.int32),
            pltpu.VMEM((1, targets), jnp.int32),
            pltpu.VMEM((1, targets), jnp.int32),
            pltpu.VMEM((2 * TAPS, OFFQ), BF16),
            pltpu.SemaphoreType.DMA((6,)),
            pltpu.SemaphoreType.DMA((2,)),
            pltpu.SemaphoreType.DMA((2, n)),
            pltpu.SemaphoreType.DMA((2, n)),
            pltpu.SemaphoreType.DMA((n,)),
            pltpu.SemaphoreType.DMA((n,)),
            pltpu.VMEM((TAPS, targets), F32),
        ],
        compiler_params=pltpu.CompilerParams(
            collective_id=0, has_side_effects=True, vmem_limit_bytes=8 << 20
        ),
    )(
        *map(
            in_hbm,
            (
                panels,
                block_phase,
                target_owner.reshape(1, targets),
                target_cell.reshape(1, targets),
                target_offset.reshape(1, targets),
                jnp.asarray(taps),
                jnp.asarray(mh),
                jnp.asarray(ml),
            ),
        )
    )
    return pl.pallas_call(
        functools.partial(product_kernel, n, order, nblk, gain),
        out_shape=(
            jax.ShapeDtypeStruct((channels, GS), F32),
            jax.ShapeDtypeStruct((channels, targets), F32),
        ),
        in_specs=[vmem] * 13,
        out_specs=(hbm, hbm),
        scratch_shapes=[
            pltpu.SemaphoreType.DMA((GS // LANES + 1,)),
            pltpu.VMEM((channels, GS), F32),
            pltpu.VMEM((channels, targets), F32),
            pltpu.VMEM((n, 2, 8, cols), F32),
            pltpu.VMEM((2 * n * channels, cols), BF16),
            pltpu.VMEM((TILES * channels, deep), BF16),
            pltpu.VMEM((TILES * channels, deep), F8),
            pltpu.VMEM((TILES * channels, deep), F8),
            pltpu.VMEM((channels, deep), BF16),
            pltpu.VMEM((channels, deep), F8),
            pltpu.VMEM((channels, deep), F8),
            pltpu.VMEM((deep, 2 * targets), BF16),
            pltpu.VMEM((deep, 2 * targets), F8),
            pltpu.VMEM((deep, 2 * targets), F8),
            pltpu.VMEM((deep, 2 * (TILE - FIRST)), BF16),
            pltpu.VMEM((deep, 2 * (TILE - FIRST)), F8),
            pltpu.VMEM((deep, 2 * (TILE - FIRST)), F8),
        ],
        compiler_params=pltpu.CompilerParams(vmem_limit_bytes=24 << 20),
    )(*ready)


def solution(mesh):
    placed = (
        P(None, "term"),
        P(None, "term"),
        P(("slab", "term"), None),
        P(("slab", "term")),
        P(("slab", "term")),
    )
    return jax.shard_map(
        functools.partial(body, mesh.shape["slab"], mesh.shape["term"]),
        mesh=mesh,
        in_specs=placed,
        out_specs=(P(None, ("slab", "term")), P(None, ("slab", "term"))),
        check_vma=False,
    )
```
